256 devices in a mesh: dp: 4 (over y), center: 64 (over x, z, core).
Axes of the slice: x: 4, y: 4, z: 8, core: 2. Of those that a mesh axis runs over, the one named last changes fastest.
Arguments:
- embeddings: bfloat16 [8192, 512], P(('dp', 'center')), may hold values from -0.59765625 to 0.59765625
- labels: int32 [8192], P(('dp', 'center')), may hold values from 0 to 10002431, as said below
- centers: bfloat16 [768, 128, 512], P('center'), may hold values from -0.25 to 0.25
- momentum: float32 [768, 128, 512], P('center'), may hold values from -6 to 6
- block_list: int32 [768], P('center'), may hold values from -1 to 78143, as said below
- counts: int32 [64], P('center'), may hold values from 4 to 12, as said below
Outputs:
- loss: float32 [8192], P(('dp', 'center'))
- embed_grad: float32 [8192, 512], P(('dp', 'center'))
- new_centers: bfloat16 [768, 128, 512], P('center')
- new_momentum: float32 [768, 128, 512], P('center')
The draws below stay inside these ranges and needn't reach their ends.
Inputs may be any that keep to these rules, and one draw needn't show every extreme that they name: Center device j has 12 slots; its first counts[j] slots are live and some device has all 12 live. `block_list`: live slot s of center device j holds a block id of j * 1221 to (j + 1) * 1221 - 1, all live ids distinct; every other slot holds -1. The block labels[b] // 128 of every label is held in a live slot.
All inputs are finite; a program needn't handle non-finite values.
Results may differ from the reference program's by a relative error of at most 0.009.
Values may be sent and summed in bfloat16 or wider, within the bound.
A program may use at most 192 MiB of HBM per device.

```python
import jax
import jax.numpy as jnp
from jax import lax

D = 512
BLK = 128
SLOTS = 12
BLOCKS_DEV = 1221
BATCH = 8192
TILES = 768
N_CENTER = 64


def joint_draw(key):
    base_key = jax.random.fold_in(key, 1234)
    sub_keys = jax.random.split(base_key, 6)
    least_live = (SLOTS + 2) // 3
    counts = jax.random.randint(sub_keys[0], (N_CENTER,), least_live, SLOTS + 1)
    full_rank = jax.random.randint(sub_keys[1], (), 0, N_CENTER)
    counts = jnp.where(jnp.arange(N_CENTER) == full_rank, SLOTS, counts).astype(jnp.int32)
    device_keys = jax.random.split(sub_keys[2], N_CENTER)
    picked = jax.vmap(lambda sub_key: jax.random.permutation(sub_key, BLOCKS_DEV)[:SLOTS])(device_keys)
    block_ids = (picked + jnp.arange(N_CENTER)[:, None] * BLOCKS_DEV).astype(jnp.int32)
    live_mask = jnp.arange(SLOTS)[None, :] < counts[:, None]
    block_list = jnp.where(live_mask, block_ids, -1).reshape(-1).astype(jnp.int32)
    owner_dev = jax.random.randint(sub_keys[3], (BATCH,), 0, N_CENTER)
    raw_draw = jax.random.randint(sub_keys[4], (BATCH,), 0, 1 << 20)
    slot_pick = raw_draw % counts[owner_dev]
    column = jax.random.randint(sub_keys[5], (BATCH,), 0, BLK)
    labels = (block_ids[owner_dev, slot_pick] * BLK + column).astype(jnp.int32)
    return (labels, block_list, counts)


def draw_labels(key, part):
    return joint_draw(key)[0]


def draw_block_list(key, part):
    return joint_draw(key)[1]


def draw_counts(key, part):
    return joint_draw(key)[2]


def shard_levels(key, dims, shards, smallest, high):
    factor_of, own = 1.0, jax.random.fold_in(key, 6)
    for position, shards_of in shards:
        draws = jnp.exp(jax.random.uniform(jax.random.fold_in(own, position), (shards_of,), jnp.float32, smallest / len(shards), high / len(shards)))
        factor_of = factor_of * jnp.repeat(draws, dims[position] // shards_of).reshape([-1 if axis == position else 1 for axis in range(len(dims))])
    return factor_of


def gaussian(key, dims, scale, most, cuts=(), kind=jnp.bfloat16):
    level = shard_levels(key, dims, cuts, -0.22, 0.18) if cuts else 1.0
    drawn = jax.random.normal(key, dims, jnp.float32) * scale * level
    return jnp.minimum(jnp.maximum(drawn, -most), most).astype(kind)


def setup_inputs(seed: int = 0) -> dict:
    seeds = jax.random.split(jax.random.key(seed), 7)
    return {
        "embeddings": gaussian(seeds[0], (BATCH, D), 0.1, 0.59765625, ((0, 256),)),
        "labels": draw_labels(jax.random.fold_in(seeds[6], 71), 0),
        "centers": gaussian(seeds[2], (TILES, BLK, D), D ** -0.5, 0.25, ((0, 64),)),
        "momentum": gaussian(seeds[3], (TILES, BLK, D), 1.0, 6.0, ((0, 64),), jnp.float32),
        "block_list": draw_block_list(jax.random.fold_in(seeds[6], 71), 0),
        "counts": draw_counts(jax.random.fold_in(seeds[6], 71), 0),
    }


logit_scale = 64.0
margin_cos = 0.35
momentum_rate = 0.9
learn_rate = 0.1
tiny_eps = 1e-06

def unit_rows(values):
    squares = lax.optimization_barrier(jnp.sum(values * values, axis=-1, keepdims=True))
    norms = jnp.sqrt(squares + tiny_eps)
    return (values / norms, norms)

def reference(embeddings, labels, centers, momentum, block_list, counts):
    x_float = embeddings.astype(jnp.float32)
    x_unit, x_norm = unit_rows(x_float)
    x_bf = x_unit.astype(jnp.bfloat16)
    label_block = labels // BLK
    label_col = labels % BLK
    col_iota = jnp.arange(BLK, dtype=jnp.int32)
    slot_iota = jnp.arange(SLOTS, dtype=jnp.int32)
    shard_w = centers.reshape(N_CENTER, SLOTS, BLK, D)
    shard_v = momentum.reshape(N_CENTER, SLOTS, BLK, D)
    shard_ids = block_list.reshape(N_CENTER, SLOTS)

    def shard_logits(w_shard, ids_shard, count_one):
        w_float = w_shard.astype(jnp.float32)
        w_unit, w_norm = unit_rows(w_float)
        w_bf = w_unit.astype(jnp.bfloat16).reshape(SLOTS * BLK, D)
        cosine = jnp.dot(x_bf, w_bf.T, preferred_element_type=jnp.float32)
        hit_mask = (ids_shard[None, :, None] == label_block[:, None, None]) & (col_iota[None, None, :] == label_col[:, None, None])
        hit_float = hit_mask.astype(jnp.float32).reshape(BATCH, SLOTS * BLK)
        live_cols = jnp.broadcast_to((slot_iota < count_one)[:, None], (SLOTS, BLK)).reshape(SLOTS * BLK)
        logit = logit_scale * cosine - logit_scale * margin_cos * hit_float
        exp_z = jnp.where(live_cols[None, :], jnp.exp(logit), 0.0)
        return (exp_z, hit_float, logit, w_float, w_unit, w_norm, w_bf)

    def first_pass(inputs):
        w_shard, ids_shard, count_one = inputs
        outs_all = shard_logits(w_shard, ids_shard, count_one)
        exp_z, hit_float, logit = (outs_all[0], outs_all[1], outs_all[2])
        return (lax.optimization_barrier(jnp.sum(exp_z, axis=1)), lax.optimization_barrier(jnp.sum(hit_float * logit, axis=1)))
    part_total, part_pos = lax.map(first_pass, (shard_w, shard_ids, counts))
    total = lax.optimization_barrier(jnp.sum(part_total, axis=0))
    pos_logit = lax.optimization_barrier(jnp.sum(part_pos, axis=0))
    loss = jnp.log(total) - pos_logit

    def second_pass(carry, inputs):
        w_shard, v_shard, ids_shard, count_one = inputs
        exp_z, hit_float, logit, w_float, w_unit, w_norm, w_bf = shard_logits(w_shard, ids_shard, count_one)
        err_bf = (logit_scale * (exp_z / total[:, None] - hit_float)).astype(jnp.bfloat16)
        carry = carry + jnp.dot(err_bf, w_bf, preferred_element_type=jnp.float32)
        grad_unit = lax.dot_general(err_bf, x_bf, (((0,), (0,)), ((), ())), preferred_element_type=jnp.float32).reshape(SLOTS, BLK, D)
        grad_w = (grad_unit - w_unit * lax.optimization_barrier(jnp.sum(w_unit * grad_unit, axis=-1, keepdims=True))) / w_norm
        live_tile = (slot_iota < count_one)[:, None, None]
        v_float = v_shard.astype(jnp.float32)
        new_v = jnp.where(live_tile, momentum_rate * v_float + grad_w, v_float)
        new_w = jnp.where(live_tile, (w_float - learn_rate * new_v).astype(jnp.bfloat16), w_shard)
        return (carry, (new_w, new_v))
    grad_x, (new_w, new_v) = lax.scan(second_pass, jnp.zeros((BATCH, D), jnp.float32), (shard_w, shard_v, shard_ids, counts))
    embed_grad = (grad_x - x_unit * lax.optimization_barrier(jnp.sum(x_unit * grad_x, axis=-1, keepdims=True))) / x_norm
    return (loss, embed_grad, new_w.reshape(TILES, BLK, D), new_v.reshape(TILES, BLK, D))
```

```python
import math

import jax
import jax.numpy as jnp
from jax import lax
from jax.experimental import pallas as pl
from jax.experimental.pallas import tpu as pltpu
from jax.sharding import PartitionSpec as P

MESH = pl.DeviceIdType.MESH
NX, NZ, NC, NY = 4, 8, 2, 4
f32, bf16, i32 = jnp.float32, jnp.bfloat16, jnp.int32

scale = 64.0
margin = 0.35
momentum_rate = 0.9
learn_rate = 0.1
tiny_eps = 1e-06
log2e = math.log2(math.e)
dead_bias = -1e30


def nt_dot(a, b):
    return lax.dot_general(a, b, (((1,), (1,)), ((), ())), preferred_element_type=f32)


def nn_dot(a, b):
    return lax.dot_general(a, b, (((1,), (0,)), ((), ())), preferred_element_type=f32)


def kernel(
    emb_ref, lab_ref, ids_ref, cnt_ref, cen_hbm, mom_hbm,
    loss_ref, eg_ref, nw_hbm, nv_hbm,
    cen, mom, wbf, wT, wn, xg, labs, labz, tgt, ez, err, tp, pp, t1, t2, p1, p2, inv,
    pt, pown, gs, rA2, rB2, rP, rM,
    gown, goth, pr, xs, xr, zs, zr,
    ldsem, stsem,
    xa_s, xa_r, la_s, la_r, lz_s, lz_r, zr_s, zr_r, sb_s, sb_r,
    t1_s, t1_r, t2_s, t2_r, p1_s, p1_r, p2_s, p2_r,
    ys_s, ys_r, yg_s, yg_r, pr_s, pr_r, xs_s, xs_r, zs_s, zs_r,
):
    rows = emb_ref.shape[0]
    width = emb_ref.shape[1]
    cols = cen.shape[0]
    quart = cols // NY
    half = quart // 2
    slots = cols // 128
    zrows = NC * NX * rows
    yy = lax.axis_index("dp")
    ce = lax.axis_index("center")
    xx = ce // (NZ * NC)
    zz = (ce // NC) % NZ
    cc = ce % NC

    def dev(y, x, z, c):
        return (y % NY, ((x % NX) * NZ + z % NZ) * NC + c)

    def copy(src, dst, ssem, rsem, to):
        return pltpu.make_async_remote_copy(
            src_ref=src, dst_ref=dst, send_sem=ssem, recv_sem=rsem, device_id=to, device_id_type=MESH
        )

    me = (yy, ce)
    sib = dev(yy, xx, zz, 1 - cc)

    def landed(dst, rsem):
        copy(dst, dst, rsem, rsem, sib).wait_recv()

    xc_peers = [(dx, dc) for dx in range(NX) for dc in range(NC) if (dx, dc) != (0, 0)]
    sends = []

    def send(src, dst, ssem, rsem, to):
        c = copy(src, dst, ssem, rsem, to)
        c.start()
        sends.append(c)

    ld_cen = pltpu.make_async_copy(cen_hbm, cen, ldsem.at[0])
    ld_mom = pltpu.make_async_copy(mom_hbm, mom, ldsem.at[1])
    ld_cen.start()
    ld_mom.start()
    barrier = pltpu.get_barrier_semaphore()
    greet = [dev(yy, xx + dx, zz, (cc + dc) % NC) for dx, dc in xc_peers]
    greet += [dev(yy, xx, zz + dz, cc) for dz in range(1, NZ)]
    greet += [dev(yy + 1, xx, zz, cc), dev(yy + NY - 1, xx, zz, cc)]
    for d in greet:
        pl.semaphore_signal(barrier, inc=1, device_id=d, device_id_type=MESH)

    xf = emb_ref[...].astype(f32)
    xn = jnp.sqrt(jnp.sum(xf * xf, axis=1, keepdims=True) + tiny_eps)
    xu = xf / xn
    xrow = pl.multiple_of(xx * rows, rows)
    xg[zz, cc, pl.ds(xrow, rows), :] = xu.astype(bf16)
    lab = lab_ref[...]
    lane = lax.broadcasted_iota(i32, (1, 128), 1)
    labs[0] = jnp.where(lane // rows == xx, lab, 0)
    pl.semaphore_wait(barrier, len(greet))

    for k in range(1, NX):
        blk = xg.at[zz, cc, pl.ds(xrow, rows), :]
        send(blk, blk, xa_s.at[k - 1], xa_r.at[k - 1], dev(yy, xx + k, zz, cc))
    for k, (dx, dc) in enumerate(xc_peers):
        send(labs.at[0], labs.at[dx * NC + dc], la_s.at[k], la_r.at[k], dev(yy, xx + dx, zz, (cc + dc) % NC))

    ld_cen.wait()

    @pl.loop(0, slots)
    def _(s):
        r = pl.ds(pl.multiple_of(s * 128, 128), 128)
        wf = cen[r, :].astype(f32)
        n = jnp.sqrt(jnp.sum(wf * wf, axis=1, keepdims=True) + tiny_eps)
        wn[r, :] = n
        wbf[r, :] = (wf * (1.0 / n)).astype(bf16)

    for k in range(1, NX):
        blk = xg.at[zz, cc, pl.ds(pl.multiple_of(((xx + NX - k) % NX) * rows, rows), rows), :]
        landed(blk, xa_r.at[k - 1])
    up, down = dev(yy, xx, zz + 1, cc), dev(yy, xx, zz + NZ - 1, cc)

    def piece(dz):
        return xg.at[(zz + dz + NZ) % NZ, cc]

    def halfpiece(dz, h):
        return xg.at[(zz + dz + NZ) % NZ, cc, pl.ds(h * 64, 64), :]

    def sib_half(dz, h, c):
        return xg.at[(zz + dz + NZ) % NZ, c, pl.ds(h * 64, 64), :]

    send(piece(0), piece(0), zr_s.at[0, 0], zr_r.at[0, 0], up)
    send(piece(0), piece(0), zr_s.at[1, 0], zr_r.at[1, 0], down)
    send(piece(0), piece(0), sb_s.at[0], sb_r.at[0], sib)

    for k, (dx, dc) in enumerate(xc_peers):
        landed(labs.at[dx * NC + dc], la_r.at[k])
    same, other = labs[0], labs[1]
    for dx in range(1, NX):
        same = same + labs[dx * NC]
        other = other + labs[dx * NC + 1]
    labz[zz, 0] = jnp.where(cc == 0, same, other)
    labz[zz, 1] = jnp.where(cc == 0, other, same)
    for dz in range(1, NZ):
        send(labz.at[zz], labz.at[zz], lz_s.at[dz - 1], lz_r.at[dz - 1], dev(yy, xx, zz + dz, cc))
    for dz in range(1, NZ):
        landed(labz.at[(zz + NZ - dz) % NZ], lz_r.at[dz - 1])
    for z in range(NZ):
        lb = jnp.concatenate([labz[z, 0], labz[z, 1]], axis=1)
        blk_id = lb // 128
        t = jnp.full(lb.shape, -1, i32)
        for s in range(slots):
            t = jnp.where(blk_id == ids_ref[s], s * 128 + lb % 128, t)
        tgt[z] = t

    live_count = cnt_ref[0]
    k2 = scale * log2e
    hit_bias = -scale * margin * log2e
    group = 4 if slots % 4 == 0 else 1

    def first_pass(dz):
        z = (zz + dz + NZ) % NZ
        xc = xg[z].reshape(zrows, width)
        tz = tgt[z]
        iota = lax.broadcasted_iota(i32, (128, zrows), 0)
        lanes = pl.ds(pl.multiple_of(z * zrows, zrows), zrows)

        def body(g, carry):
            tot, pos = carry
            r0 = pl.multiple_of(g * (group * 128), 128)
            s = nt_dot(wbf[pl.ds(r0, group * 128), :], xc)
            for u in range(group):
                slot = g * group + u
                su = s[u * 128:(u + 1) * 128]
                hit = iota == (tz - slot * 128)
                bias = jnp.where(slot < live_count, 0.0, dead_bias)
                e = jnp.exp2(su * k2 + jnp.where(hit, hit_bias, bias))
                ez[pl.ds(r0 + u * 128, 128), lanes] = e
                tot = tot + jnp.sum(e, axis=0, keepdims=True)
                pos = pos + jnp.sum(jnp.where(hit, su, 0.0), axis=0, keepdims=True)
            return tot, pos

        zero = jnp.zeros((1, zrows), f32)
        tot, pos = lax.fori_loop(0, slots // group, body, (zero, zero))
        tp[pl.ds(z, 1), :] = tot
        pp[pl.ds(z, 1), :] = pos

    def sib_piece(dz):
        return xg.at[(zz + dz + NZ) % NZ, 1 - cc]

    landed(sib_piece(0), sb_r.at[0])
    first_pass(0)
    for hop in range(1, NZ // 2):
        for way, to, sign in ((0, up, -1), (1, down, 1)):
            p = piece(sign * hop)
            landed(p, zr_r.at[way, hop - 1])
            if hop < NZ // 2 - 1:
                send(p, p, zr_s.at[way, hop], zr_r.at[way, hop], to)
            else:
                hp = halfpiece(sign * hop, way)
                send(hp, hp, zr_s.at[way, hop], zr_r.at[way, hop], to)
            k = 2 * hop - 1 + way
            send(p, p, sb_s.at[k], sb_r.at[k], sib)
        for way, sign in ((0, -1), (1, 1)):
            landed(sib_piece(sign * hop), sb_r.at[2 * hop - 1 + way])
            first_pass(sign * hop)
    far = NZ // 2
    for way, sign in ((0, -1), (1, 1)):
        hp = halfpiece(sign * far, way)
        landed(hp, zr_r.at[way, far - 1])
        k = 2 * far - 1 + way
        send(hp, hp, sb_s.at[k], sb_r.at[k], sib)

    @pl.loop(0, slots)
    def _(s):
        c0 = pl.multiple_of(s * 128, 128)
        wT[:, pl.ds(c0, 128)] = wbf[pl.ds(c0, 128), :].T

    for way, sign in ((0, -1), (1, 1)):
        landed(sib_half(sign * far, way, 1 - cc), sb_r.at[2 * far - 1 + way])
    first_pass(far)

    def reduce_plane(part, first, second, s1, r1, s2, r2):
        for k, (dx, dc) in enumerate(xc_peers):
            send(part, first.at[k], s1.at[k], r1.at[k], dev(yy, xx + dx, zz, (cc + dc) % NC))

        def middle():
            acc = part[...]
            for k in range(len(xc_peers)):
                landed(first.at[k], r1.at[k])
                acc = acc + first[k]
            second[0] = acc
            for dz in range(1, NZ):
                send(second.at[0], second.at[dz], s2.at[dz - 1], r2.at[dz - 1], dev(yy, xx, zz + dz, cc))

        def last():
            acc = second[0]
            for dz in range(1, NZ):
                landed(second.at[dz], r2.at[dz - 1])
                acc = acc + second[dz]
            return acc

        return middle, last

    tot_mid, tot_last = reduce_plane(tp, t1, t2, t1_s, t1_r, t2_s, t2_r)
    pos_mid, pos_last = reduce_plane(pp, p1, p2, p1_s, p1_r, p2_s, p2_r)
    tot_mid()
    pos_mid()
    total = tot_last()
    inv[...] = scale / total

    def errors(q):
        @pl.loop(0, NZ)
        def _(z):
            lanes = pl.ds(pl.multiple_of(z * zrows, zrows), zrows)
            iota = lax.broadcasted_iota(i32, (128, zrows), 0)
            iz = inv[pl.ds(z, 1), :]
            tz = tgt[z]
            for u in range(quart // 128):
                r0 = pl.multiple_of(q * quart + u * 128, 128)
                hit = iota == (tz - r0)
                e = ez[pl.ds(r0, 128), lanes] * iz - jnp.where(hit, scale, 0.0)
                err[pl.ds(r0, 128), lanes] = e.astype(bf16)

    def center_grad(q):
        r0 = pl.multiple_of(q * quart, 128)
        return nn_dot(err[pl.ds(r0, quart), :], xg[...].reshape(NZ * zrows, width))

    yup, ydn = dev(yy + 1, xx, zz, cc), dev(yy + NY - 1, xx, zz, cc)
    q2, qp, qm = (yy + 2) % NY, (yy + 1) % NY, (yy + NY - 1) % NY

    errors(q2)
    g = center_grad(q2).astype(bf16)
    pt[0, 0] = g[:half]
    pt[0, 1] = g[half:]
    send(pt.at[0, 0], rA2, ys_s.at[0], ys_r.at[0], yup)
    send(pt.at[0, 1], rB2, ys_s.at[1], ys_r.at[1], ydn)
    errors(qp)
    g = center_grad(qp)
    pt[1, 1] = g[half:].astype(bf16)
    send(pt.at[1, 1], rP.at[1], ys_s.at[2], ys_r.at[2], yup)
    gA = g[:half]
    landed(rA2, ys_r.at[0])
    pt[1, 0] = (gA + rA2[...].astype(f32)).astype(bf16)
    send(pt.at[1, 0], rP.at[0], ys_s.at[3], ys_r.at[3], yup)
    errors(qm)
    g = center_grad(qm)
    pt[2, 0] = g[:half].astype(bf16)
    send(pt.at[2, 0], rM.at[0], ys_s.at[4], ys_r.at[4], ydn)
    landed(rB2, ys_r.at[1])
    pt[2, 1] = (g[half:] + rB2[...].astype(f32)).astype(bf16)
    send(pt.at[2, 1], rM.at[1], ys_s.at[5], ys_r.at[5], ydn)
    errors(yy)
    pown[...] = center_grad(yy)

    @pl.loop(0, NZ)
    def _(z):
        lanes = pl.ds(pl.multiple_of(z * zrows, zrows), zrows)
        gt = nn_dot(wT[...], err[:, lanes])
        gx = gt.T
        lo, hi = gx[: zrows // 2], gx[zrows // 2:]
        gown[z] = jnp.where(cc == 0, lo, hi)
        goth[z] = jnp.where(cc == 0, hi, lo).astype(bf16)

    send(goth, pr, pr_s.at[0], pr_r.at[0], sib)

    def own_half(h):
        landed(rP.at[h], ys_r.at[3 - h])
        landed(rM.at[h], ys_r.at[4 + h])
        s = pown[pl.ds(h * half, half), :] + rP[h].astype(f32) + rM[h].astype(f32)
        gs[yy, h] = s.astype(bf16)
        send(gs.at[yy, h], gs.at[yy, h], yg_s.at[h], yg_r.at[h], yup)
        send(gs.at[yy, h], gs.at[yy, h], yg_s.at[2 + h], yg_r.at[2 + h], ydn)

    landed(pr, pr_r.at[0])

    @pl.loop(0, NZ)
    def _(z):
        h = gown[z] + pr[z].astype(f32)
        gown[z] = h
        for x in range(NX):
            xs[x, z] = h[x * rows:(x + 1) * rows].astype(bf16)

    for k in range(1, NX):
        send(xs.at[(xx + k) % NX], xr.at[k - 1], xs_s.at[k - 1], xs_r.at[k - 1], dev(yy, xx + k, zz, cc))

    own_half(0)
    own_half(1)

    ld_mom.wait()
    tile = 64
    stores = []

    def update(q, h, k):
        @pl.loop(0, half // tile)
        def _(i):
            r0 = pl.multiple_of(q * quart + h * half + i * tile, tile)
            r = pl.ds(r0, tile)
            g = gs[q, h, pl.ds(pl.multiple_of(i * tile, tile), tile), :].astype(f32)
            wb = cen[r, :]
            wf = wb.astype(f32)
            rn = 1.0 / wn[r, :]
            wu = wf * rn
            gw = (g - wu * jnp.sum(wu * g, axis=1, keepdims=True)) * rn
            live = (r0 // 128) < live_count
            v = mom[r, :]
            nv = jnp.where(live, momentum_rate * v + gw, v)
            nw = jnp.where(live, wf - learn_rate * nv, wf).astype(bf16)
            mom[r, :] = nv
            cen[r, :] = nw

        r = pl.ds(pl.multiple_of(q * quart + h * half, tile), half)
        for j, (src, dst) in enumerate(((cen, nw_hbm), (mom, nv_hbm))):
            c = pltpu.make_async_copy(src.at[r, :], dst.at[r, :], stsem.at[k, j])
            c.start()
            stores.append(c)

    update(yy, 0, 0)
    update(yy, 1, 1)

    landed(gs.at[qm, 0], yg_r.at[0])
    send(gs.at[qm, 0], gs.at[qm, 0], yg_s.at[4], yg_r.at[4], yup)
    landed(gs.at[qp, 1], yg_r.at[3])
    send(gs.at[qp, 1], gs.at[qp, 1], yg_s.at[5], yg_r.at[5], ydn)

    for k in range(1, NX):
        landed(xr.at[k - 1], xs_r.at[k - 1])
    for z in range(NZ):
        h = gown[z, pl.ds(xrow, rows), :]
        for k in range(1, NX):
            h = h + xr[k - 1, z].astype(f32)
        gown[z, pl.ds(xrow, rows), :] = h
        zs[z] = h.astype(bf16)
    for dz in range(1, NZ):
        send(zs.at[(zz + dz) % NZ], zr.at[dz - 1], zs_s.at[dz - 1], zs_r.at[dz - 1], dev(yy, xx, zz + dz, cc))

    landed(gs.at[qm, 1], yg_r.at[1])
    landed(gs.at[qp, 0], yg_r.at[2])
    update(qm, 0, 2)
    update(qm, 1, 3)
    update(qp, 0, 4)
    update(qp, 1, 5)

    gx = gown[zz, pl.ds(xrow, rows), :]
    for dz in range(1, NZ):
        landed(zr.at[dz - 1], zs_r.at[dz - 1])
        gx = gx + zr[dz - 1].astype(f32)
    eg_ref[...] = (gx - xu * jnp.sum(xu * gx, axis=1, keepdims=True)) / xn
    pos = pos_last()
    all_loss = jnp.log(scale / inv[...]) - (scale * pos - scale * margin)
    inv[...] = all_loss
    line = inv[pl.ds(zz, 1), :]
    mine = jnp.zeros((1, rows), f32)
    for c in range(NC):
        for x in range(NX):
            at = (c * NX + x) * rows
            here = jnp.logical_and(cc == c, xx == x)
            mine = jnp.where(here, line[:, at:at + rows], mine)
    loss_ref[...] = mine

    landed(gs.at[q2, 0], yg_r.at[4])
    update(q2, 0, 6)
    landed(gs.at[q2, 1], yg_r.at[5])
    update(q2, 1, 7)

    for c in sends:
        c.wait_send()
    for c in stores:
        c.wait()


def on_device(embeddings, labels, centers, momentum, block_list, counts):
    rows, width = embeddings.shape
    slots, blk, _ = centers.shape
    cols = slots * blk
    zrows = NC * NX * rows
    group = NZ * zrows
    quart = cols // NY
    half = quart // 2
    vm, dma = pltpu.VMEM, pltpu.SemaphoreType.DMA
    npeer = NX * NC - 1
    scratch = [
        vm((cols, width), bf16),
        vm((cols, width), f32),
        vm((cols, width), bf16),
        vm((width, cols), bf16),
        vm((cols, 1), f32),
        vm((NZ, NC, NX * rows, width), bf16),
        vm((NX * NC, 1, 128), i32),
        vm((NZ, NC, 1, 128), i32),
        vm((NZ, 1, zrows), i32),
        vm((cols, group), f32),
        vm((cols, group), bf16),
        vm((NZ, zrows), f32),
        vm((NZ, zrows), f32),
        vm((npeer, NZ, zrows), f32),
        vm((NZ, NZ, zrows), f32),
        vm((npeer, NZ, zrows), f32),
        vm((NZ, NZ, zrows), f32),
        vm((NZ, zrows), f32),
        vm((NY - 1, 2, half, width), bf16),
        vm((quart, width), f32),
        vm((NY, 2, half, width), bf16),
        vm((half, width), bf16),
        vm((half, width), bf16),
        vm((2, half, width), bf16),
        vm((2, half, width), bf16),
        vm((NZ, NX * rows, width), f32),
        vm((NZ, NX * rows, width), bf16),
        vm((NZ, NX * rows, width), bf16),
        vm((NX, NZ, rows, width), bf16),
        vm((NX - 1, NZ, rows, width), bf16),
        vm((NZ, rows, width), bf16),
        vm((NZ - 1, rows, width), bf16),
        dma((2,)), dma((8, 2)),
        dma((NX - 1,)), dma((NX - 1,)), dma((npeer,)), dma((npeer,)), dma((NZ - 1,)), dma((NZ - 1,)),
        dma((2, NZ // 2)), dma((2, NZ // 2)), dma((NZ + 1,)), dma((NZ + 1,)),
        dma((npeer,)), dma((npeer,)), dma((NZ - 1,)), dma((NZ - 1,)),
        dma((npeer,)), dma((npeer,)), dma((NZ - 1,)), dma((NZ - 1,)),
        dma((6,)), dma((6,)), dma((6,)), dma((6,)), dma((1,)), dma((1,)),
        dma((NX - 1,)), dma((NX - 1,)), dma((NZ - 1,)), dma((NZ - 1,)),
    ]
    vmem = pl.BlockSpec(memory_space=pltpu.VMEM)
    smem = pl.BlockSpec(memory_space=pltpu.SMEM)
    hbm = pl.BlockSpec(memory_space=pl.ANY)
    loss, eg, nw, nv = pl.pallas_call(
        kernel,
        out_shape=(
            jax.ShapeDtypeStruct((1, rows), f32),
            jax.ShapeDtypeStruct((rows, width), f32),
            jax.ShapeDtypeStruct((cols, width), bf16),
            jax.ShapeDtypeStruct((cols, width), f32),
        ),
        in_specs=[vmem, vmem, smem, smem, hbm, hbm],
        out_specs=(vmem, vmem, hbm, hbm),
        scratch_shapes=scratch,
        compiler_params=pltpu.CompilerParams(
            collective_id=0, has_side_effects=True, vmem_limit_bytes=62 * 1024 * 1024
        ),
        name="margin_step",
    )(
        embeddings,
        jnp.tile(labels, 128 // rows).reshape(1, 128),
        block_list,
        counts,
        centers.reshape(cols, width),
        momentum.reshape(cols, width),
    )
    return (
        loss.reshape(rows),
        eg,
        nw.reshape(centers.shape),
        nv.reshape(momentum.shape),
    )


def solution(mesh):
    return jax.shard_map(
        on_device,
        mesh=mesh,
        in_specs=(
            P(("dp", "center"), None),
            P(("dp", "center")),
            P("center", None, None),
            P("center", None, None),
            P("center"),
            P("center"),
        ),
        out_specs=(
            P(("dp", "center")),
            P(("dp", "center"), None),
            P("center", None, None),
            P("center", None, None),
        ),
        check_vma=False,
    )
```

```python
import math

import jax
import jax.numpy as jnp
from jax import lax
from jax.experimental import pallas as pl
from jax.experimental.pallas import tpu as pltpu
from jax.sharding import PartitionSpec as P

MESH = pl.DeviceIdType.MESH
NX, NZ, NC, NY = 4, 8, 2, 4
f32, bf16, i32 = jnp.float32, jnp.bfloat16, jnp.int32

scale = 64.0
margin = 0.35
momentum_rate = 0.9
learn_rate = 0.1
tiny_eps = 1e-06
log2e = math.log2(math.e)
dead_bias = -1e30


def nt_dot(a, b):
    return lax.dot_general(a, b, (((1,), (1,)), ((), ())), preferred_element_type=f32)


def nn_dot(a, b):
    return lax.dot_general(a, b, (((1,), (0,)), ((), ())), preferred_element_type=f32)


def kernel(
    emb_ref, lab_ref, ids_ref, cnt_ref, cen_hbm, mom_hbm,
    loss_ref, eg_ref, nw_hbm, nv_hbm,
    cen, mom, wbf, wT, wn, xg, labs, labz, tgt, ez, err, tp, pp, t1, t2, p1, p2, inv,
    pt, pf, gs, r2, rP, rM,
    gown, goth, pr, xs, xr, zs, zr,
    ldsem, stsem,
    xa_s, xa_r, la_s, la_r, lz_s, lz_r, zg_s, zg_r, sb_s, sb_r,
    t1_s, t1_r, t2_s, t2_r, p1_s, p1_r, p2_s, p2_r,
    ys_s, ys_r, yg_s, yg_r, pr_s, pr_r, xs_s, xs_r, zs_s, zs_r,
):
    rows = emb_ref.shape[0]
    width = emb_ref.shape[1]
    cols = cen.shape[0]
    quart = cols // NY
    piece = quart // 4
    slots = cols // 128
    zrows = NC * NX * rows
    yy = lax.axis_index("dp")
    ce = lax.axis_index("center")
    xx = ce // (NZ * NC)
    zz = (ce // NC) % NZ
    cc = ce % NC

    def dev(y, x, z, c):
        return (y % NY, ((x % NX) * NZ + z % NZ) * NC + c)

    def copy(src, dst, ssem, rsem, to):
        return pltpu.make_async_remote_copy(
            src_ref=src, dst_ref=dst, send_sem=ssem, recv_sem=rsem, device_id=to, device_id_type=MESH
        )

    me = (yy, ce)
    sib = dev(yy, xx, zz, 1 - cc)

    def landed(dst, rsem):
        copy(dst, dst, rsem, rsem, sib).wait_recv()

    xc_peers = [(dx, dc) for dx in range(NX) for dc in range(NC) if (dx, dc) != (0, 0)]
    sends = []

    def send(src, dst, ssem, rsem, to):
        c = copy(src, dst, ssem, rsem, to)
        c.start()
        sends.append(c)

    ld_cen = pltpu.make_async_copy(cen_hbm, cen, ldsem.at[0])
    ld_mom = pltpu.make_async_copy(mom_hbm, mom, ldsem.at[1])
    ld_cen.start()
    ld_mom.start()
    barrier = pltpu.get_barrier_semaphore()
    greet = [dev(yy, xx + dx, zz, (cc + dc) % NC) for dx, dc in xc_peers]
    greet += [dev(yy, xx, zz + dz, cc) for dz in range(1, NZ)]
    greet += [dev(yy + 1, xx, zz, cc), dev(yy + NY - 1, xx, zz, cc)]
    for d in greet:
        pl.semaphore_signal(barrier, inc=1, device_id=d, device_id_type=MESH)

    xf = emb_ref[...].astype(f32)
    xn = jnp.sqrt(jnp.sum(xf * xf, axis=1, keepdims=True) + tiny_eps)
    xu = xf / xn
    xrow = pl.multiple_of(xx * rows, rows)
    xg[zz, cc, pl.ds(xrow, rows), :] = xu.astype(bf16)
    lab = jnp.concatenate([lab_ref[...]] * NX, axis=1)
    lane = lax.broadcasted_iota(i32, (1, 128), 1)
    labs[0] = jnp.where(lane // rows == xx, lab, 0)
    pl.semaphore_wait(barrier, len(greet))

    def block(dz, dx):
        return xg.at[(zz + NZ - dz) % NZ, cc, pl.ds(pl.multiple_of(((xx + NX - dx) % NX) * rows, rows), rows), :]

    def along_x(dz):
        for k in (1, 3, 2):
            send(block(dz, 0), block(dz, 0), xa_s.at[dz, k - 1], xa_r.at[dz, k - 1], dev(yy, xx + k, zz, cc))

    for dz in (1, 7, 2, 6, 3, 5, 4):
        send(block(0, 0), block(0, 0), zg_s.at[dz - 1], zg_r.at[dz - 1], dev(yy, xx, zz + dz, cc))
    along_x(0)
    for k, (dx, dc) in enumerate(xc_peers):
        send(labs.at[0], labs.at[dx * NC + dc], la_s.at[k], la_r.at[k], dev(yy, xx + dx, zz, (cc + dc) % NC))

    ld_cen.wait()

    @pl.loop(0, slots)
    def _(s):
        r = pl.ds(pl.multiple_of(s * 128, 128), 128)
        wf = cen[r, :].astype(f32)
        n = jnp.sqrt(jnp.sum(wf * wf, axis=1, keepdims=True) + tiny_eps)
        wn[r, :] = n
        wbf[r, :] = (wf * (1.0 / n)).astype(bf16)

    def forward(dz):
        landed(block(dz, 0), zg_r.at[dz - 1])
        along_x(dz)

    def share(dz):
        for k in (1, 3, 2):
            landed(block(dz, k), xa_r.at[dz, k - 1])
        p = xg.at[(zz + NZ - dz) % NZ, cc]
        send(p, p, sb_s.at[dz], sb_r.at[dz], sib)

    forward(1)
    forward(7)
    share(0)

    for k, (dx, dc) in enumerate(xc_peers):
        landed(labs.at[dx * NC + dc], la_r.at[k])
    same, other = labs[0], labs[1]
    for dx in range(1, NX):
        same = same + labs[dx * NC]
        other = other + labs[dx * NC + 1]
    labz[zz, 0] = jnp.where(cc == 0, same, other)
    labz[zz, 1] = jnp.where(cc == 0, other, same)
    for dz in (1, 7, 2, 6, 3, 5, 4):
        send(labz.at[zz], labz.at[zz], lz_s.at[dz - 1], lz_r.at[dz - 1], dev(yy, xx, zz + dz, cc))

    def targets(z):
        lb = jnp.concatenate([labz[z, 0], labz[z, 1]], axis=1)
        blk_id = lb // 128
        t = jnp.full(lb.shape, -1, i32)
        for s in range(slots):
            t = jnp.where(blk_id == ids_ref[s], s * 128 + lb % 128, t)
        tgt[z] = t
        return t

    live_count = cnt_ref[0]
    k2 = scale * log2e
    hit_bias = -scale * margin * log2e
    group = 4 if slots % 4 == 0 else 1

    def first_pass(dz):
        z = (zz + NZ - dz) % NZ
        landed(xg.at[z, 1 - cc], sb_r.at[dz])
        if dz:
            landed(labz.at[z], lz_r.at[dz - 1])
        xc = xg[z].reshape(zrows, width)
        tz = targets(z)
        iota = lax.broadcasted_iota(i32, (128, zrows), 0)
        lanes = pl.ds(pl.multiple_of(z * zrows, zrows), zrows)

        def body(g, carry):
            tot, pos = carry
            r0 = pl.multiple_of(g * (group * 128), 128)
            s = nt_dot(wbf[pl.ds(r0, group * 128), :], xc)
            for u in range(group):
                slot = g * group + u
                su = s[u * 128:(u + 1) * 128]
                hit = iota == (tz - slot * 128)
                bias = jnp.where(slot < live_count, 0.0, dead_bias)
                e = jnp.exp2(su * k2 + jnp.where(hit, hit_bias, bias))
                ez[pl.ds(r0 + u * 128, 128), lanes] = e
                tot = tot + jnp.sum(e, axis=0, keepdims=True)
                pos = pos + jnp.sum(jnp.where(hit, su, 0.0), axis=0, keepdims=True)
            return tot, pos

        zero = jnp.zeros((1, zrows), f32)
        tot, pos = lax.fori_loop(0, slots // group, body, (zero, zero))
        tp[pl.ds(z, 1), :] = tot
        pp[pl.ds(z, 1), :] = pos

    forward(2)
    forward(6)
    first_pass(0)
    share(1)
    share(7)
    forward(3)
    forward(5)
    forward(4)
    first_pass(1)
    first_pass(7)
    share(2)
    share(6)
    first_pass(2)
    first_pass(6)
    share(3)
    share(5)
    share(4)
    first_pass(3)
    first_pass(5)

    @pl.loop(0, slots)
    def _(s):
        c0 = pl.multiple_of(s * 128, 128)
        wT[:, pl.ds(c0, 128)] = wbf[pl.ds(c0, 128), :].T

    first_pass(4)

    def reduce_plane(part, first, second, s1, r1, s2, r2):
        for k, (dx, dc) in enumerate(xc_peers):
            send(part, first.at[k], s1.at[k], r1.at[k], dev(yy, xx + dx, zz, (cc + dc) % NC))

        def middle():
            acc = part[...]
            for k in range(len(xc_peers)):
                landed(first.at[k], r1.at[k])
                acc = acc + first[k]
            second[0] = acc
            for dz in range(1, NZ):
                send(second.at[0], second.at[dz], s2.at[dz - 1], r2.at[dz - 1], dev(yy, xx, zz + dz, cc))

        def last():
            acc = second[0]
            for dz in range(1, NZ):
                landed(second.at[dz], r2.at[dz - 1])
                acc = acc + second[dz]
            return acc

        return middle, last

    tot_mid, tot_last = reduce_plane(tp, t1, t2, t1_s, t1_r, t2_s, t2_r)
    tot_mid()
    total = tot_last()
    inv[...] = scale / total

    def errors(q):
        @pl.loop(0, NZ)
        def _(z):
            lanes = pl.ds(pl.multiple_of(z * zrows, zrows), zrows)
            iota = lax.broadcasted_iota(i32, (128, zrows), 0)
            iz = inv[pl.ds(z, 1), :]
            tz = tgt[z]
            for u in range(quart // 128):
                r0 = pl.multiple_of(q * quart + u * 128, 128)
                hit = iota == (tz - r0)
                e = ez[pl.ds(r0, 128), lanes] * iz - jnp.where(hit, scale, 0.0)
                err[pl.ds(r0, 128), lanes] = e.astype(bf16)

    def center_grad(q):
        r0 = pl.multiple_of(q * quart, 128)
        return nn_dot(err[pl.ds(r0, quart), :], xg[...].reshape(NZ * zrows, width))

    yup, ydn = dev(yy + 1, xx, zz, cc), dev(yy + NY - 1, xx, zz, cc)
    q2, qp, qm = (yy + 2) % NY, (yy + 1) % NY, (yy + NY - 1) % NY

    def to_y(src, dst, k, to):
        send(src, dst, ys_s.at[k], ys_r.at[k], to)

    def keep(q, slot):
        g = center_grad(q)
        for p in range(4):
            pt[slot, p] = g[p * piece:(p + 1) * piece].astype(bf16)
        return g

    errors(q2)
    keep(q2, 0)
    for n in range(2):
        to_y(pt.at[0, n], r2.at[n], n, yup)
        to_y(pt.at[0, 2 + n], r2.at[2 + n], 2 + n, ydn)
    errors(qp)
    pf[0] = center_grad(qp)
    for n in range(2):
        pt[1, 2 + n] = pf[0, pl.ds((2 + n) * piece, piece), :].astype(bf16)
    to_y(pt.at[1, 2], rP.at[2], 4, yup)
    errors(qm)
    pf[1] = center_grad(qm)
    for n in range(2):
        pt[2, n] = pf[1, pl.ds(n * piece, piece), :].astype(bf16)
    to_y(pt.at[2, 0], rM.at[0], 5, ydn)
    errors(yy)

    def merge(n):
        landed(r2.at[n], ys_r.at[n])
        pt[1, n] = (pf[0, pl.ds(n * piece, piece), :] + r2[n].astype(f32)).astype(bf16)
        to_y(pt.at[1, n], rP.at[n], 6 + n, yup)
        landed(r2.at[2 + n], ys_r.at[2 + n])
        pt[2, 2 + n] = (pf[1, pl.ds((2 + n) * piece, piece), :] + r2[2 + n].astype(f32)).astype(bf16)
        to_y(pt.at[2, 2 + n], rM.at[2 + n], 8 + n, ydn)

    def own(n):
        for p in (n, 2 + n):
            landed(rP.at[p], ys_r.at[(6 + n) if p < 2 else (4 if n == 0 else 10)])
            landed(rM.at[p], ys_r.at[(8 + n) if p >= 2 else (5 if n == 0 else 11)])
            s = pf[2, pl.ds(p * piece, piece), :] + rP[p].astype(f32) + rM[p].astype(f32)
            gs[yy, p] = s.astype(bf16)
        for p, q in ((n, 2 + n),):
            send(gs.at[yy, p], gs.at[yy, p], yg_s.at[0, p], yg_r.at[0, p], yup)
            send(gs.at[yy, q], gs.at[yy, q], yg_s.at[1, q], yg_r.at[1, q], ydn)
            send(gs.at[yy, q], gs.at[yy, q], yg_s.at[0, q], yg_r.at[0, q], yup)
            send(gs.at[yy, p], gs.at[yy, p], yg_s.at[1, p], yg_r.at[1, p], ydn)

    def onward(n):
        landed(gs.at[qm, n], yg_r.at[0, n])
        send(gs.at[qm, n], gs.at[qm, n], yg_s.at[2, n], yg_r.at[2, n], yup)
        landed(gs.at[qp, 2 + n], yg_r.at[1, 2 + n])
        send(gs.at[qp, 2 + n], gs.at[qp, 2 + n], yg_s.at[2, 2 + n], yg_r.at[2, 2 + n], ydn)

    group2 = NZ // 2

    def row_grad(lo, hi):
        @pl.loop(lo, hi)
        def _(i):
            z = (zz + NZ // 2 + i) % NZ
            lanes = pl.ds(pl.multiple_of(z * zrows, zrows), zrows)
            gx = nn_dot(wT[...], err[:, lanes]).T
            a, b = gx[: zrows // 2], gx[zrows // 2:]
            gown[i] = jnp.where(cc == 0, a, b)
            goth[i] = jnp.where(cc == 0, b, a).astype(bf16)

    def pair(g):
        part = pl.ds(g * group2, group2)
        send(goth.at[part], pr.at[part], pr_s.at[g], pr_r.at[g], sib)

    def rows_x(g):
        part = pl.ds(g * group2, group2)
        landed(pr.at[part], pr_r.at[g])

        @pl.loop(0, group2)
        def _(n):
            i = g * group2 + n
            h = gown[i] + pr[i].astype(f32)
            gown[i] = h
            for x in range(NX):
                xs[g, x, n] = h[x * rows:(x + 1) * rows].astype(bf16)

        for k in (1, 3, 2):
            send(xs.at[g, (xx + k) % NX], xr.at[g, k - 1], xs_s.at[g, k - 1], xs_r.at[g, k - 1], dev(yy, xx + k, zz, cc))

    def rows_z(g):
        for k in range(1, NX):
            landed(xr.at[g, k - 1], xs_r.at[g, k - 1])
        for n in range(group2):
            i = g * group2 + n
            dz = (NZ // 2 + i) % NZ
            h = gown[i, pl.ds(xrow, rows), :]
            for k in range(1, NX):
                h = h + xr[g, k - 1, n].astype(f32)
            if dz == 0:
                gown[i, pl.ds(xrow, rows), :] = h
            else:
                zs[i] = h.astype(bf16)
                send(zs.at[i], zr.at[dz - 1], zs_s.at[dz - 1], zs_r.at[dz - 1], dev(yy, xx, zz + dz, cc))

    pos_mid, pos_last = reduce_plane(pp, p1, p2, p1_s, p1_r, p2_s, p2_r)
    merge(0)
    to_y(pt.at[1, 3], rP.at[3], 10, yup)
    to_y(pt.at[2, 1], rM.at[1], 11, ydn)
    row_grad(0, group2)
    pair(0)
    merge(1)
    pf[2] = center_grad(yy)
    rows_x(0)
    row_grad(group2, group2 + 2)
    own(0)
    row_grad(group2 + 2, NZ)
    pair(1)
    pos_mid()
    own(1)
    rows_x(1)

    ld_mom.wait()
    tile = 32
    stores = []

    def update(q, p0, np, k):
        base = q * quart + p0 * piece

        @pl.loop(0, np * piece // tile)
        def _(i):
            at = pl.multiple_of(i * tile, tile)
            r0 = pl.multiple_of(base + at, tile)
            r = pl.ds(r0, tile)
            g = gs[q, p0 + at // piece, pl.ds(pl.multiple_of(at % piece, tile), tile), :].astype(f32)
            wf = cen[r, :].astype(f32)
            rn = 1.0 / wn[r, :]
            wu = wf * rn
            gw = (g - wu * jnp.sum(wu * g, axis=1, keepdims=True)) * rn
            live = (r0 // 128) < live_count
            v = mom[r, :]
            nv = jnp.where(live, momentum_rate * v + gw, v)
            nw = jnp.where(live, wf - learn_rate * nv, wf).astype(bf16)
            mom[r, :] = nv
            cen[r, :] = nw

        r = pl.ds(pl.multiple_of(base, tile), np * piece)
        for j, (src, dst) in enumerate(((cen, nw_hbm), (mom, nv_hbm))):
            c = pltpu.make_async_copy(src.at[r, :], dst.at[r, :], stsem.at[k, j])
            c.start()
            stores.append(c)

    update(yy, 0, 4, 0)
    onward(0)
    rows_z(0)
    onward(1)
    rows_z(1)
    for n in range(2):
        landed(gs.at[qm, 2 + n], yg_r.at[0, 2 + n])
        landed(gs.at[qp, n], yg_r.at[1, n])
    update(qm, 0, 4, 1)
    update(qp, 0, 4, 2)

    gx = gown[NZ // 2, pl.ds(xrow, rows), :]
    for dz in range(1, NZ):
        landed(zr.at[dz - 1], zs_r.at[dz - 1])
        gx = gx + zr[dz - 1].astype(f32)
    eg_ref[...] = (gx - xu * jnp.sum(xu * gx, axis=1, keepdims=True)) / xn
    pos = pos_last()
    all_loss = jnp.log(scale / inv[...]) - (scale * pos - scale * margin)
    inv[...] = all_loss
    line = inv[pl.ds(zz, 1), :]
    mine = jnp.zeros((1, rows), f32)
    for c in range(NC):
        for x in range(NX):
            at = (c * NX + x) * rows
            here = jnp.logical_and(cc == c, xx == x)
            mine = jnp.where(here, line[:, at:at + rows], mine)
    loss_ref[...] = mine

    for n in range(2):
        landed(gs.at[q2, n], yg_r.at[2, n])
        landed(gs.at[q2, 2 + n], yg_r.at[2, 2 + n])
    update(q2, 0, 4, 3)

    for c in sends:
        c.wait_send()
    for c in stores:
        c.wait()


def on_device(embeddings, labels, centers, momentum, block_list, counts):
    rows, width = embeddings.shape
    slots, blk, _ = centers.shape
    cols = slots * blk
    zrows = NC * NX * rows
    group = NZ * zrows
    quart = cols // NY
    piece = quart // 4
    vm, dma = pltpu.VMEM, pltpu.SemaphoreType.DMA
    npeer = NX * NC - 1
    scratch = [
        vm((cols, width), bf16),
        vm((cols, width), f32),
        vm((cols, width), bf16),
        vm((width, cols), bf16),
        vm((cols, 1), f32),
        vm((NZ, NC, NX * rows, width), bf16),
        vm((NX * NC, 1, 128), i32),
        vm((NZ, NC, 1, 128), i32),
        vm((NZ, 1, zrows), i32),
        vm((cols, group), f32),
        vm((cols, group), bf16),
        vm((NZ, zrows), f32),
        vm((NZ, zrows), f32),
        vm((npeer, NZ, zrows), f32),
        vm((NZ, NZ, zrows), f32),
        vm((npeer, NZ, zrows), f32),
        vm((NZ, NZ, zrows), f32),
        vm((NZ, zrows), f32),
        vm((3, 4, piece, width), bf16),
        vm((3, quart, width), f32),
        vm((NY, 4, piece, width), bf16),
        vm((4, piece, width), bf16),
        vm((4, piece, width), bf16),
        vm((4, piece, width), bf16),
        vm((NZ, NX * rows, width), f32),
        vm((NZ, NX * rows, width), bf16),
        vm((NZ, NX * rows, width), bf16),
        vm((2, NX, NZ // 2, rows, width), bf16),
        vm((2, NX - 1, NZ // 2, rows, width), bf16),
        vm((NZ, rows, width), bf16),
        vm((NZ - 1, rows, width), bf16),
        dma((2,)), dma((4, 2)),
        dma((NZ, NX - 1)), dma((NZ, NX - 1)), dma((npeer,)), dma((npeer,)), dma((NZ - 1,)), dma((NZ - 1,)),
        dma((NZ - 1,)), dma((NZ - 1,)), dma((NZ,)), dma((NZ,)),
        dma((npeer,)), dma((npeer,)), dma((NZ - 1,)), dma((NZ - 1,)),
        dma((npeer,)), dma((npeer,)), dma((NZ - 1,)), dma((NZ - 1,)),
        dma((12,)), dma((12,)), dma((3, 4)), dma((3, 4)), dma((2,)), dma((2,)),
        dma((2, NX - 1)), dma((2, NX - 1)), dma((NZ - 1,)), dma((NZ - 1,)),
    ]
    vmem = pl.BlockSpec(memory_space=pltpu.VMEM)
    smem = pl.BlockSpec(memory_space=pltpu.SMEM)
    hbm = pl.BlockSpec(memory_space=pl.ANY)
    loss, eg, nw, nv = pl.pallas_call(
        kernel,
        out_shape=(
            jax.ShapeDtypeStruct((1, rows), f32),
            jax.ShapeDtypeStruct((rows, width), f32),
            jax.ShapeDtypeStruct((cols, width), bf16),
            jax.ShapeDtypeStruct((cols, width), f32),
        ),
        in_specs=[vmem, vmem, smem, smem, hbm, hbm],
        out_specs=(vmem, vmem, hbm, hbm),
        scratch_shapes=scratch,
        compiler_params=pltpu.CompilerParams(
            collective_id=0, has_side_effects=True, vmem_limit_bytes=62 * 1024 * 1024
        ),
        name="margin_step",
    )(
        embeddings,
        labels.reshape(1, rows),
        block_list,
        counts,
        centers.reshape(cols, width),
        momentum.reshape(cols, width),
    )
    return (
        loss.reshape(rows),
        eg,
        nw.reshape(centers.shape),
        nv.reshape(momentum.shape),
    )


def solution(mesh):
    return jax.shard_map(
        on_device,
        mesh=mesh,
        in_specs=(
            P(("dp", "center"), None),
            P(("dp", "center")),
            P("center", None, None),
            P("center", None, None),
            P("center"),
            P("center"),
        ),
        out_specs=(
            P(("dp", "center")),
            P(("dp", "center"), None),
            P("center", None, None),
            P("center", None, None),
        ),
        check_vma=False,
    )
```

```python
import math

import jax
import jax.numpy as jnp
from jax import lax
from jax.experimental import pallas as pl
from jax.experimental.pallas import tpu as pltpu
from jax.sharding import PartitionSpec as P

MESH = pl.DeviceIdType.MESH
NX, NZ, NC, NY = 4, 8, 2, 4
f32, bf16, i32 = jnp.float32, jnp.bfloat16, jnp.int32

scale = 64.0
margin = 0.35
momentum_rate = 0.9
learn_rate = 0.1
tiny_eps = 1e-06
log2e = math.log2(math.e)
dead_bias = -1e30


def nt_dot(a, b):
    return lax.dot_general(a, b, (((1,), (1,)), ((), ())), preferred_element_type=f32)


def nn_dot(a, b):
    return lax.dot_general(a, b, (((1,), (0,)), ((), ())), preferred_element_type=f32)


def kernel(
    emb_ref, lab_ref, ids_ref, cnt_ref, cen_hbm, mom_hbm,
    loss_ref, eg_ref, nw_hbm, nv_hbm,
    cen, mom, wbf, wT, wn, xg, labs, labz, tgt, ez, err, tp, pp, t1, t2, p1, p2, inv,
    pt, pf, gs, r2, rP, rM,
    gown, goth, pr, xs, xr, zs, zr,
    ldsem, stsem,
    xa_s, xa_r, xz_s, xz_r, la_s, la_r, lz_s, lz_r, zg_s, zg_r, sb_s, sb_r,
    t1_s, t1_r, t2_s, t2_r, p1_s, p1_r, p2_s, p2_r,
    ys_s, ys_r, yg_s, yg_r, pr_s, pr_r, xs_s, xs_r, zs_s, zs_r,
):
    rows = emb_ref.shape[0]
    width = emb_ref.shape[1]
    cols = cen.shape[0]
    quart = cols // NY
    piece = quart // 4
    slots = cols // 128
    zrows = NC * NX * rows
    yy = lax.axis_index("dp")
    ce = lax.axis_index("center")
    xx = ce // (NZ * NC)
    zz = (ce // NC) % NZ
    cc = ce % NC

    def dev(y, x, z, c):
        return (y % NY, ((x % NX) * NZ + z % NZ) * NC + c)

    def copy(src, dst, ssem, rsem, to):
        return pltpu.make_async_remote_copy(
            src_ref=src, dst_ref=dst, send_sem=ssem, recv_sem=rsem, device_id=to, device_id_type=MESH
        )

    me = (yy, ce)
    sib = dev(yy, xx, zz, 1 - cc)

    def landed(dst, rsem):
        copy(dst, dst, rsem, rsem, sib).wait_recv()

    xc_peers = [(dx, dc) for dx in range(NX) for dc in range(NC) if (dx, dc) != (0, 0)]
    sends = []

    def send(src, dst, ssem, rsem, to):
        c = copy(src, dst, ssem, rsem, to)
        c.start()
        sends.append(c)

    ld_cen = pltpu.make_async_copy(cen_hbm, cen, ldsem.at[0])
    ld_mom = pltpu.make_async_copy(mom_hbm, mom, ldsem.at[1])
    ld_cen.start()
    ld_mom.start()
    barrier = pltpu.get_barrier_semaphore()
    greet = [dev(yy, xx + dx, zz, (cc + dc) % NC) for dx, dc in xc_peers]
    greet += [dev(yy, xx, zz + dz, cc) for dz in range(1, NZ)]
    greet += [dev(yy + 1, xx, zz, cc), dev(yy + NY - 1, xx, zz, cc)]
    for d in greet:
        pl.semaphore_signal(barrier, inc=1, device_id=d, device_id_type=MESH)

    xf = emb_ref[...].astype(f32)
    xn = jnp.sqrt(jnp.sum(xf * xf, axis=1, keepdims=True) + tiny_eps)
    xu = xf / xn
    xrow = pl.multiple_of(xx * rows, rows)
    xg[zz, cc, pl.ds(xrow, rows), :] = xu.astype(bf16)
    lab = jnp.concatenate([lab_ref[...]] * NX, axis=1)
    lane = lax.broadcasted_iota(i32, (1, 128), 1)
    labs[0] = jnp.where(lane // rows == xx, lab, 0)
    pl.semaphore_wait(barrier, len(greet))

    def block(dz, dx):
        return xg.at[(zz + NZ - dz) % NZ, cc, pl.ds(pl.multiple_of(((xx + NX - dx) % NX) * rows, rows), rows), :]

    def along_x(dz):
        for k in (1, 3, 2):
            send(block(dz, 0), block(dz, 0), xa_s.at[dz, k - 1], xa_r.at[dz, k - 1], dev(yy, xx + k, zz, cc))

    def along_z(*steps):
        for dz in steps:
            send(block(0, 0), block(0, 0), zg_s.at[dz - 1], zg_r.at[dz - 1], dev(yy, xx, zz + dz, cc))

    along_z(2, 6)
    along_x(0)
    along_z(1, 7)
    for k, (dx, dc) in enumerate(xc_peers):
        send(labs.at[0], labs.at[dx * NC + dc], la_s.at[k], la_r.at[k], dev(yy, xx + dx, zz, (cc + dc) % NC))

    ld_cen.wait()

    @pl.loop(0, slots)
    def _(s):
        r = pl.ds(pl.multiple_of(s * 128, 128), 128)
        wf = cen[r, :].astype(f32)
        n = jnp.sqrt(jnp.sum(wf * wf, axis=1, keepdims=True) + tiny_eps)
        wn[r, :] = n
        wbf[r, :] = (wf * (1.0 / n)).astype(bf16)

    along_z(3, 5, 4)

    def forward(dz):
        landed(block(dz, 0), zg_r.at[dz - 1])
        along_x(dz)

    def neighbours():
        for k in (1, 3, 2):
            landed(block(0, k), xa_r.at[0, k - 1])
            for w, dz in ((0, 1), (1, NZ - 1)):
                send(block(0, k), block(0, k), xz_s.at[w, k - 1], xz_r.at[w, k - 1], dev(yy, xx, zz + dz, cc))

    def share(dz):
        if dz in (1, NZ - 1):
            landed(block(dz, 0), zg_r.at[dz - 1])
        for k in (1, 3, 2):
            if dz in (1, NZ - 1):
                landed(block(dz, k), xz_r.at[int(dz != 1), k - 1])
            elif dz:
                landed(block(dz, k), xa_r.at[dz, k - 1])
        p = xg.at[(zz + NZ - dz) % NZ, cc]
        send(p, p, sb_s.at[dz], sb_r.at[dz], sib)

    neighbours()
    share(0)

    for k, (dx, dc) in enumerate(xc_peers):
        landed(labs.at[dx * NC + dc], la_r.at[k])
    same, other = labs[0], labs[1]
    for dx in range(1, NX):
        same = same + labs[dx * NC]
        other = other + labs[dx * NC + 1]
    labz[zz, 0] = jnp.where(cc == 0, same, other)
    labz[zz, 1] = jnp.where(cc == 0, other, same)
    for dz in (1, 7, 2, 6, 3, 5, 4):
        send(labz.at[zz], labz.at[zz], lz_s.at[dz - 1], lz_r.at[dz - 1], dev(yy, xx, zz + dz, cc))

    def targets(z):
        lb = jnp.concatenate([labz[z, 0], labz[z, 1]], axis=1)
        blk_id = lb // 128
        t = jnp.full(lb.shape, -1, i32)
        for s in range(slots):
            t = jnp.where(blk_id == ids_ref[s], s * 128 + lb % 128, t)
        tgt[z] = t
        return t

    live_count = cnt_ref[0]
    k2 = scale * log2e
    hit_bias = -scale * margin * log2e
    group = 4 if slots % 4 == 0 else 1

    def first_pass(dz):
        z = (zz + NZ - dz) % NZ
        landed(xg.at[z, 1 - cc], sb_r.at[dz])
        if dz:
            landed(labz.at[z], lz_r.at[dz - 1])
        xc = xg[z].reshape(zrows, width)
        tz = targets(z)
        iota = lax.broadcasted_iota(i32, (128, zrows), 0)
        lanes = pl.ds(pl.multiple_of(z * zrows, zrows), zrows)

        def body(g, carry):
            tot, pos = carry
            r0 = pl.multiple_of(g * (group * 128), 128)
            s = nt_dot(wbf[pl.ds(r0, group * 128), :], xc)
            for u in range(group):
                slot = g * group + u
                su = s[u * 128:(u + 1) * 128]
                hit = iota == (tz - slot * 128)
                bias = jnp.where(slot < live_count, 0.0, dead_bias)
                e = jnp.exp2(su * k2 + jnp.where(hit, hit_bias, bias))
                ez[pl.ds(r0 + u * 128, 128), lanes] = e
                tot = tot + jnp.sum(e, axis=0, keepdims=True)
                pos = pos + jnp.sum(jnp.where(hit, su, 0.0), axis=0, keepdims=True)
            return tot, pos

        zero = jnp.zeros((1, zrows), f32)
        tot, pos = lax.fori_loop(0, slots // group, body, (zero, zero))
        tp[pl.ds(z, 1), :] = tot
        pp[pl.ds(z, 1), :] = pos

    forward(2)
    forward(6)
    first_pass(0)
    forward(3)
    forward(5)
    forward(4)
    share(1)
    share(7)
    first_pass(1)
    share(2)
    share(6)
    first_pass(7)
    first_pass(2)
    share(3)
    share(5)
    first_pass(6)
    share(4)
    first_pass(3)
    first_pass(5)
    first_pass(4)

    def reduce_plane(part, first, second, s1, r1, s2, r2):
        for k, (dx, dc) in enumerate(xc_peers):
            send(part, first.at[k], s1.at[k], r1.at[k], dev(yy, xx + dx, zz, (cc + dc) % NC))

        def middle():
            acc = part[...]
            for k in range(len(xc_peers)):
                landed(first.at[k], r1.at[k])
                acc = acc + first[k]
            second[0] = acc
            for dz in range(1, NZ):
                send(second.at[0], second.at[dz], s2.at[dz - 1], r2.at[dz - 1], dev(yy, xx, zz + dz, cc))

        def last():
            acc = second[0]
            for dz in range(1, NZ):
                landed(second.at[dz], r2.at[dz - 1])
                acc = acc + second[dz]
            return acc

        return middle, last

    tot_mid, tot_last = reduce_plane(tp, t1, t2, t1_s, t1_r, t2_s, t2_r)

    @pl.loop(0, slots)
    def _(s):
        c0 = pl.multiple_of(s * 128, 128)
        wT[:, pl.ds(c0, 128)] = wbf[pl.ds(c0, 128), :].T

    tot_mid()
    total = tot_last()
    inv[...] = scale / total

    def errors(q):
        @pl.loop(0, NZ)
        def _(z):
            lanes = pl.ds(pl.multiple_of(z * zrows, zrows), zrows)
            iota = lax.broadcasted_iota(i32, (128, zrows), 0)
            iz = inv[pl.ds(z, 1), :]
            tz = tgt[z]
            for u in range(quart // 128):
                r0 = pl.multiple_of(q * quart + u * 128, 128)
                hit = iota == (tz - r0)
                e = ez[pl.ds(r0, 128), lanes] * iz - jnp.where(hit, scale, 0.0)
                err[pl.ds(r0, 128), lanes] = e.astype(bf16)

    def center_grad(q):
        r0 = pl.multiple_of(q * quart, 128)
        return nn_dot(err[pl.ds(r0, quart), :], xg[...].reshape(NZ * zrows, width))

    yup, ydn = dev(yy + 1, xx, zz, cc), dev(yy + NY - 1, xx, zz, cc)
    q2, qp, qm = (yy + 2) % NY, (yy + 1) % NY, (yy + NY - 1) % NY

    def to_y(src, dst, k, to):
        send(src, dst, ys_s.at[k], ys_r.at[k], to)

    def keep(q, slot):
        g = center_grad(q)
        for p in range(4):
            pt[slot, p] = g[p * piece:(p + 1) * piece].astype(bf16)
        return g

    errors(q2)
    keep(q2, 0)
    for n in range(2):
        to_y(pt.at[0, n], r2.at[n], n, yup)
        to_y(pt.at[0, 2 + n], r2.at[2 + n], 2 + n, ydn)
    errors(qp)
    pf[0] = center_grad(qp)
    for n in range(2):
        pt[1, 2 + n] = pf[0, pl.ds((2 + n) * piece, piece), :].astype(bf16)
    to_y(pt.at[1, 2], rP.at[2], 4, yup)
    errors(qm)
    pf[1] = center_grad(qm)
    for n in range(2):
        pt[2, n] = pf[1, pl.ds(n * piece, piece), :].astype(bf16)
    to_y(pt.at[2, 0], rM.at[0], 5, ydn)
    errors(yy)

    def merge(n):
        landed(r2.at[n], ys_r.at[n])
        pt[1, n] = (pf[0, pl.ds(n * piece, piece), :] + r2[n].astype(f32)).astype(bf16)
        to_y(pt.at[1, n], rP.at[n], 6 + n, yup)
        landed(r2.at[2 + n], ys_r.at[2 + n])
        pt[2, 2 + n] = (pf[1, pl.ds((2 + n) * piece, piece), :] + r2[2 + n].astype(f32)).astype(bf16)
        to_y(pt.at[2, 2 + n], rM.at[2 + n], 8 + n, ydn)

    def own(n):
        for p in (n, 2 + n):
            landed(rP.at[p], ys_r.at[(6 + n) if p < 2 else (4 if n == 0 else 10)])
            landed(rM.at[p], ys_r.at[(8 + n) if p >= 2 else (5 if n == 0 else 11)])
            s = pf[2, pl.ds(p * piece, piece), :] + rP[p].astype(f32) + rM[p].astype(f32)
            gs[yy, p] = s.astype(bf16)
        for p, q in ((n, 2 + n),):
            send(gs.at[yy, p], gs.at[yy, p], yg_s.at[0, p], yg_r.at[0, p], yup)
            send(gs.at[yy, q], gs.at[yy, q], yg_s.at[1, q], yg_r.at[1, q], ydn)
            send(gs.at[yy, q], gs.at[yy, q], yg_s.at[0, q], yg_r.at[0, q], yup)
            send(gs.at[yy, p], gs.at[yy, p], yg_s.at[1, p], yg_r.at[1, p], ydn)

    def onward(n):
        landed(gs.at[qm, n], yg_r.at[0, n])
        send(gs.at[qm, n], gs.at[qm, n], yg_s.at[2, n], yg_r.at[2, n], yup)
        landed(gs.at[qp, 2 + n], yg_r.at[1, 2 + n])
        send(gs.at[qp, 2 + n], gs.at[qp, 2 + n], yg_s.at[2, 2 + n], yg_r.at[2, 2 + n], ydn)

    group2 = NZ // 2

    def row_grad(lo, hi):
        @pl.loop(lo, hi)
        def _(i):
            z = (zz + NZ // 2 + i) % NZ
            lanes = pl.ds(pl.multiple_of(z * zrows, zrows), zrows)
            gx = nn_dot(wT[...], err[:, lanes]).T
            a, b = gx[: zrows // 2], gx[zrows // 2:]
            gown[i] = jnp.where(cc == 0, a, b)
            goth[i] = jnp.where(cc == 0, b, a).astype(bf16)

    def pair(g):
        part = pl.ds(g * group2, group2)
        send(goth.at[part], pr.at[part], pr_s.at[g], pr_r.at[g], sib)

    def rows_x(g):
        part = pl.ds(g * group2, group2)
        landed(pr.at[part], pr_r.at[g])

        @pl.loop(0, group2)
        def _(n):
            i = g * group2 + n
            h = gown[i] + pr[i].astype(f32)
            gown[i] = h
            for x in range(NX):
                xs[g, x, n] = h[x * rows:(x + 1) * rows].astype(bf16)

        for k in (1, 3, 2):
            send(xs.at[g, (xx + k) % NX], xr.at[g, k - 1], xs_s.at[g, k - 1], xs_r.at[g, k - 1], dev(yy, xx + k, zz, cc))

    def rows_z(g):
        for k in range(1, NX):
            landed(xr.at[g, k - 1], xs_r.at[g, k - 1])
        for n in range(group2):
            i = g * group2 + n
            dz = (NZ // 2 + i) % NZ
            h = gown[i, pl.ds(xrow, rows), :]
            for k in range(1, NX):
                h = h + xr[g, k - 1, n].astype(f32)
            if dz == 0:
                gown[i, pl.ds(xrow, rows), :] = h
            else:
                zs[i] = h.astype(bf16)
                send(zs.at[i], zr.at[dz - 1], zs_s.at[dz - 1], zs_r.at[dz - 1], dev(yy, xx, zz + dz, cc))

    pos_mid, pos_last = reduce_plane(pp, p1, p2, p1_s, p1_r, p2_s, p2_r)
    merge(0)
    to_y(pt.at[1, 3], rP.at[3], 10, yup)
    to_y(pt.at[2, 1], rM.at[1], 11, ydn)
    row_grad(0, group2)
    pair(0)
    merge(1)
    pf[2] = center_grad(yy)
    rows_x(0)
    row_grad(group2, group2 + 2)
    own(0)
    row_grad(group2 + 2, NZ)
    pair(1)
    pos_mid()
    own(1)
    rows_x(1)

    ld_mom.wait()
    tile = 32
    stores = []

    def update(q, p0, np, k):
        base = q * quart + p0 * piece

        @pl.loop(0, np * piece // tile)
        def _(i):
            at = pl.multiple_of(i * tile, tile)
            r0 = pl.multiple_of(base + at, tile)
            r = pl.ds(r0, tile)
            g = gs[q, p0 + at // piece, pl.ds(pl.multiple_of(at % piece, tile), tile), :].astype(f32)
            wf = cen[r, :].astype(f32)
            rn = 1.0 / wn[r, :]
            wu = wf * rn
            gw = (g - wu * jnp.sum(wu * g, axis=1, keepdims=True)) * rn
            live = (r0 // 128) < live_count
            v = mom[r, :]
            nv = jnp.where(live, momentum_rate * v + gw, v)
            nw = jnp.where(live, wf - learn_rate * nv, wf).astype(bf16)
            mom[r, :] = nv
            cen[r, :] = nw

        r = pl.ds(pl.multiple_of(base, tile), np * piece)
        for j, (src, dst) in enumerate(((cen, nw_hbm), (mom, nv_hbm))):
            c = pltpu.make_async_copy(src.at[r, :], dst.at[r, :], stsem.at[k, j])
            c.start()
            stores.append(c)

    update(yy, 0, 4, 0)
    onward(0)
    rows_z(0)
    onward(1)
    rows_z(1)
    for n in range(2):
        landed(gs.at[qm, 2 + n], yg_r.at[0, 2 + n])
        landed(gs.at[qp, n], yg_r.at[1, n])
    update(qm, 0, 4, 1)
    update(qp, 0, 4, 2)

    gx = gown[NZ // 2, pl.ds(xrow, rows), :]
    for dz in range(1, NZ):
        landed(zr.at[dz - 1], zs_r.at[dz - 1])
        gx = gx + zr[dz - 1].astype(f32)
    eg_ref[...] = (gx - xu * jnp.sum(xu * gx, axis=1, keepdims=True)) / xn
    pos = pos_last()
    all_loss = jnp.log(scale / inv[...]) - (scale * pos - scale * margin)
    inv[...] = all_loss
    line = inv[pl.ds(zz, 1), :]
    mine = jnp.zeros((1, rows), f32)
    for c in range(NC):
        for x in range(NX):
            at = (c * NX + x) * rows
            here = jnp.logical_and(cc == c, xx == x)
            mine = jnp.where(here, line[:, at:at + rows], mine)
    loss_ref[...] = mine

    for n in range(2):
        landed(gs.at[q2, n], yg_r.at[2, n])
        landed(gs.at[q2, 2 + n], yg_r.at[2, 2 + n])
    update(q2, 0, 4, 3)

    for c in sends:
        c.wait_send()
    for c in stores:
        c.wait()


def store_kernel(*refs):
    n = len(refs) // 2
    ins, outs, sem = refs[:n], refs[n:2 * n], refs[2 * n]
    copies = [pltpu.make_async_copy(a, b, sem.at[k]) for k, (a, b) in enumerate(zip(ins, outs))]
    for c in copies:
        c.start()
    for c in copies:
        c.wait()


def on_device(embeddings, labels, centers, momentum, block_list, counts):
    rows, width = embeddings.shape
    slots, blk, _ = centers.shape
    cols = slots * blk
    zrows = NC * NX * rows
    group = NZ * zrows
    quart = cols // NY
    piece = quart // 4
    vm, dma = pltpu.VMEM, pltpu.SemaphoreType.DMA
    npeer = NX * NC - 1
    scratch = [
        vm((cols, width), bf16),
        vm((cols, width), f32),
        vm((cols, width), bf16),
        vm((width, cols), bf16),
        vm((cols, 1), f32),
        vm((NZ, NC, NX * rows, width), bf16),
        vm((NX * NC, 1, 128), i32),
        vm((NZ, NC, 1, 128), i32),
        vm((NZ, 1, zrows), i32),
        vm((cols, group), f32),
        vm((cols, group), bf16),
        vm((NZ, zrows), f32),
        vm((NZ, zrows), f32),
        vm((npeer, NZ, zrows), f32),
        vm((NZ, NZ, zrows), f32),
        vm((npeer, NZ, zrows), f32),
        vm((NZ, NZ, zrows), f32),
        vm((NZ, zrows), f32),
        vm((3, 4, piece, width), bf16),
        vm((3, quart, width), f32),
        vm((NY, 4, piece, width), bf16),
        vm((4, piece, width), bf16),
        vm((4, piece, width), bf16),
        vm((4, piece, width), bf16),
        vm((NZ, NX * rows, width), f32),
        vm((NZ, NX * rows, width), bf16),
        vm((NZ, NX * rows, width), bf16),
        vm((2, NX, NZ // 2, rows, width), bf16),
        vm((2, NX - 1, NZ // 2, rows, width), bf16),
        vm((NZ, rows, width), bf16),
        vm((NZ - 1, rows, width), bf16),
        dma((2,)), dma((4, 2)),
        dma((NZ, NX - 1)), dma((NZ, NX - 1)), dma((2, NX - 1)), dma((2, NX - 1)), dma((npeer,)), dma((npeer,)), dma((NZ - 1,)), dma((NZ - 1,)),
        dma((NZ - 1,)), dma((NZ - 1,)), dma((NZ,)), dma((NZ,)),
        dma((npeer,)), dma((npeer,)), dma((NZ - 1,)), dma((NZ - 1,)),
        dma((npeer,)), dma((npeer,)), dma((NZ - 1,)), dma((NZ - 1,)),
        dma((12,)), dma((12,)), dma((3, 4)), dma((3, 4)), dma((2,)), dma((2,)),
        dma((2, NX - 1)), dma((2, NX - 1)), dma((NZ - 1,)), dma((NZ - 1,)),
    ]
    vmem = pl.BlockSpec(memory_space=pltpu.VMEM)
    smem = pl.BlockSpec(memory_space=pltpu.SMEM)
    hbm = pl.BlockSpec(memory_space=pltpu.HBM)
    place = pl.BlockSpec(memory_space=pl.ANY)
    results = pl.pallas_call(
        kernel,
        out_shape=(
            jax.ShapeDtypeStruct((1, rows), f32),
            jax.ShapeDtypeStruct((rows, width), f32),
            jax.ShapeDtypeStruct((cols, width), bf16),
            jax.ShapeDtypeStruct((cols, width), f32),
        ),
        in_specs=[vmem, vmem, smem, smem, hbm, hbm],
        out_specs=(vmem, vmem, place, place),
        scratch_shapes=scratch,
        compiler_params=pltpu.CompilerParams(
            collective_id=0, has_side_effects=True, vmem_limit_bytes=44 * 1024 * 1024
        ),
        name="margin_step",
    )(
        embeddings,
        labels.reshape(1, rows),
        block_list,
        counts,
        pltpu.with_memory_space_constraint(centers.reshape(cols, width), pltpu.HBM),
        pltpu.with_memory_space_constraint(momentum.reshape(cols, width), pltpu.HBM),
    )
    loss, eg, nw, nv = pl.pallas_call(
        store_kernel,
        out_shape=tuple(jax.ShapeDtypeStruct(r.shape, r.dtype) for r in results),
        in_specs=[place] * len(results),
        out_specs=(hbm,) * len(results),
        scratch_shapes=[dma((len(results),))],
        compiler_params=pltpu.CompilerParams(vmem_limit_bytes=1024 * 1024),
        name="store_results",
    )(*results)
    return (
        loss.reshape(rows),
        eg,
        nw.reshape(centers.shape),
        nv.reshape(momentum.shape),
    )


def solution(mesh):
    return jax.shard_map(
        on_device,
        mesh=mesh,
        in_specs=(
            P(("dp", "center"), None),
            P(("dp", "center")),
            P("center", None, None),
            P("center", None, None),
            P("center"),
            P("center"),
        ),
        out_specs=(
            P(("dp", "center")),
            P(("dp", "center"), None),
            P("center", None, None),
            P("center", None, None),
        ),
        check_vma=False,
    )
```

```python
import math

import jax
import jax.numpy as jnp
from jax import lax
from jax.experimental import pallas as pl
from jax.experimental.pallas import tpu as pltpu
from jax.sharding import PartitionSpec as P

MESH = pl.DeviceIdType.MESH
NX, NZ, NC, NY = 4, 8, 2, 4
f32, bf16, i32 = jnp.float32, jnp.bfloat16, jnp.int32

scale = 64.0
margin = 0.35
momentum_rate = 0.9
learn_rate = 0.1
tiny_eps = 1e-06
log2e = math.log2(math.e)
dead_bias = -1e30


def nt_dot(a, b):
    return lax.dot_general(a, b, (((1,), (1,)), ((), ())), preferred_element_type=f32)


def nn_dot(a, b):
    return lax.dot_general(a, b, (((1,), (0,)), ((), ())), preferred_element_type=f32)


def kernel(
    emb_hbm, lab_hbm, ids_hbm, cnt_ref, cen_hbm, mom_hbm,
    loss_ref, eg_ref, nw_hbm, nv_hbm,
    emb_ref, lab_ref, ids_ref, cen, mom, wbf, wT, wn, xg, labs, labz, tgt, ez, err, tp, pp, t1, t2, p1, p2, inv,
    pt, pf, gs, r2, rP, rM,
    gown, goth, pr, xs, xr, zs, zr,
    ldsem, stsem,
    xa_s, xa_r, xz_s, xz_r, la_s, la_r, lz_s, lz_r, zg_s, zg_r, sb_s, sb_r,
    t1_s, t1_r, t2_s, t2_r, p1_s, p1_r, p2_s, p2_r,
    ys_s, ys_r, yg_s, yg_r, pr_s, pr_r, xs_s, xs_r, zs_s, zs_r,
):
    rows = emb_ref.shape[0]
    width = emb_ref.shape[1]
    cols = cen.shape[0]
    quart = cols // NY
    piece = quart // 4
    slots = cols // 128
    zrows = NC * NX * rows
    yy = lax.axis_index("dp")
    ce = lax.axis_index("center")
    xx = ce // (NZ * NC)
    zz = (ce // NC) % NZ
    cc = ce % NC

    def dev(y, x, z, c):
        return (y % NY, ((x % NX) * NZ + z % NZ) * NC + c)

    def copy(src, dst, ssem, rsem, to):
        return pltpu.make_async_remote_copy(
            src_ref=src, dst_ref=dst, send_sem=ssem, recv_sem=rsem, device_id=to, device_id_type=MESH
        )

    me = (yy, ce)
    sib = dev(yy, xx, zz, 1 - cc)

    def landed(dst, rsem):
        copy(dst, dst, rsem, rsem, sib).wait_recv()

    xc_peers = [(dx, dc) for dx in range(NX) for dc in range(NC) if (dx, dc) != (0, 0)]
    sends = []

    def send(src, dst, ssem, rsem, to):
        c = copy(src, dst, ssem, rsem, to)
        c.start()
        sends.append(c)

    ld_cen = pltpu.make_async_copy(cen_hbm, cen, ldsem.at[0])
    ld_mom = pltpu.make_async_copy(mom_hbm, mom, ldsem.at[1])
    small = [
        pltpu.make_async_copy(a, b, ldsem.at[2 + k])
        for k, (a, b) in enumerate(
            ((emb_hbm, emb_ref), (lab_hbm, lab_ref), (ids_hbm, ids_ref))
        )
    ]
    for c in small:
        c.start()
    ld_cen.start()
    ld_mom.start()
    barrier = pltpu.get_barrier_semaphore()
    greet = [dev(yy, xx + dx, zz, (cc + dc) % NC) for dx, dc in xc_peers]
    greet += [dev(yy, xx, zz + dz, cc) for dz in range(1, NZ)]
    greet += [dev(yy + 1, xx, zz, cc), dev(yy + NY - 1, xx, zz, cc)]
    for d in greet:
        pl.semaphore_signal(barrier, inc=1, device_id=d, device_id_type=MESH)

    for c in small:
        c.wait()
    xf = emb_ref[...].astype(f32)
    xn = jnp.sqrt(jnp.sum(xf * xf, axis=1, keepdims=True) + tiny_eps)
    xu = xf / xn
    xrow = pl.multiple_of(xx * rows, rows)
    xg[zz, cc, pl.ds(xrow, rows), :] = xu.astype(bf16)
    lab = jnp.concatenate([lab_ref[...]] * NX, axis=1)
    lane = lax.broadcasted_iota(i32, (1, 128), 1)
    labs[0] = jnp.where(lane // rows == xx, lab, 0)
    pl.semaphore_wait(barrier, len(greet))

    def block(dz, dx):
        return xg.at[(zz + NZ - dz) % NZ, cc, pl.ds(pl.multiple_of(((xx + NX - dx) % NX) * rows, rows), rows), :]

    def along_x(dz):
        for k in (1, 3, 2):
            send(block(dz, 0), block(dz, 0), xa_s.at[dz, k - 1], xa_r.at[dz, k - 1], dev(yy, xx + k, zz, cc))

    def along_z(*steps):
        for dz in steps:
            send(block(0, 0), block(0, 0), zg_s.at[dz - 1], zg_r.at[dz - 1], dev(yy, xx, zz + dz, cc))

    along_z(2, 6)
    along_x(0)
    along_z(1, 7)
    for k, (dx, dc) in enumerate(xc_peers):
        send(labs.at[0], labs.at[dx * NC + dc], la_s.at[k], la_r.at[k], dev(yy, xx + dx, zz, (cc + dc) % NC))

    ld_cen.wait()

    @pl.loop(0, slots)
    def _(s):
        r = pl.ds(pl.multiple_of(s * 128, 128), 128)
        wf = cen[r, :].astype(f32)
        n = jnp.sqrt(jnp.sum(wf * wf, axis=1, keepdims=True) + tiny_eps)
        wn[r, :] = n
        wbf[r, :] = (wf * (1.0 / n)).astype(bf16)

    along_z(3, 5, 4)

    def forward(dz):
        landed(block(dz, 0), zg_r.at[dz - 1])
        along_x(dz)

    def neighbours():
        for k in (1, 3, 2):
            landed(block(0, k), xa_r.at[0, k - 1])
            for w, dz in ((0, 1), (1, NZ - 1)):
                send(block(0, k), block(0, k), xz_s.at[w, k - 1], xz_r.at[w, k - 1], dev(yy, xx, zz + dz, cc))

    def share(dz):
        if dz in (1, NZ - 1):
            landed(block(dz, 0), zg_r.at[dz - 1])
        for k in (1, 3, 2):
            if dz in (1, NZ - 1):
                landed(block(dz, k), xz_r.at[int(dz != 1), k - 1])
            elif dz:
                landed(block(dz, k), xa_r.at[dz, k - 1])
        p = xg.at[(zz + NZ - dz) % NZ, cc]
        send(p, p, sb_s.at[dz], sb_r.at[dz], sib)

    neighbours()
    share(0)

    for k, (dx, dc) in enumerate(xc_peers):
        landed(labs.at[dx * NC + dc], la_r.at[k])
    same, other = labs[0], labs[1]
    for dx in range(1, NX):
        same = same + labs[dx * NC]
        other = other + labs[dx * NC + 1]
    labz[zz, 0] = jnp.where(cc == 0, same, other)
    labz[zz, 1] = jnp.where(cc == 0, other, same)
    for dz in (1, 7, 2, 6, 3, 5, 4):
        send(labz.at[zz], labz.at[zz], lz_s.at[dz - 1], lz_r.at[dz - 1], dev(yy, xx, zz + dz, cc))

    def targets(z):
        lb = jnp.concatenate([labz[z, 0], labz[z, 1]], axis=1)
        blk_id = lb // 128
        t = jnp.full(lb.shape, -1, i32)
        for s in range(slots):
            t = jnp.where(blk_id == ids_ref[s], s * 128 + lb % 128, t)
        tgt[z] = t
        return t

    live_count = cnt_ref[0]
    k2 = scale * log2e
    hit_bias = -scale * margin * log2e
    group = 4 if slots % 4 == 0 else 1

    def first_pass(dz):
        z = (zz + NZ - dz) % NZ
        landed(xg.at[z, 1 - cc], sb_r.at[dz])
        if dz:
            landed(labz.at[z], lz_r.at[dz - 1])
        xc = xg[z].reshape(zrows, width)
        tz = targets(z)
        iota = lax.broadcasted_iota(i32, (128, zrows), 0)
        lanes = pl.ds(pl.multiple_of(z * zrows, zrows), zrows)

        def body(g, carry):
            tot, pos = carry
            r0 = pl.multiple_of(g * (group * 128), 128)
            s = nt_dot(wbf[pl.ds(r0, group * 128), :], xc)
            for u in range(group):
                slot = g * group + u
                su = s[u * 128:(u + 1) * 128]
                hit = iota == (tz - slot * 128)
                bias = jnp.where(slot < live_count, 0.0, dead_bias)
                e = jnp.exp2(su * k2 + jnp.where(hit, hit_bias, bias))
                ez[pl.ds(r0 + u * 128, 128), lanes] = e
                tot = tot + jnp.sum(e, axis=0, keepdims=True)
                pos = pos + jnp.sum(jnp.where(hit, su, 0.0), axis=0, keepdims=True)
            return tot, pos

        zero = jnp.zeros((1, zrows), f32)
        tot, pos = lax.fori_loop(0, slots // group, body, (zero, zero))
        tp[pl.ds(z, 1), :] = tot
        pp[pl.ds(z, 1), :] = pos

    forward(2)
    forward(6)
    first_pass(0)
    forward(3)
    forward(5)
    forward(4)
    share(1)
    share(7)
    first_pass(1)
    share(2)
    share(6)
    first_pass(7)
    first_pass(2)
    share(3)
    share(5)
    first_pass(6)
    share(4)
    first_pass(3)
    first_pass(5)
    first_pass(4)

    def reduce_plane(part, first, second, s1, r1, s2, r2):
        for k, (dx, dc) in enumerate(xc_peers):
            send(part, first.at[k], s1.at[k], r1.at[k], dev(yy, xx + dx, zz, (cc + dc) % NC))

        def middle():
            acc = part[...]
            for k in range(len(xc_peers)):
                landed(first.at[k], r1.at[k])
                acc = acc + first[k]
            second[0] = acc
            for dz in range(1, NZ):
                send(second.at[0], second.at[dz], s2.at[dz - 1], r2.at[dz - 1], dev(yy, xx, zz + dz, cc))

        def last():
            acc = second[0]
            for dz in range(1, NZ):
                landed(second.at[dz], r2.at[dz - 1])
                acc = acc + second[dz]
            return acc

        return middle, last

    tot_mid, tot_last = reduce_plane(tp, t1, t2, t1_s, t1_r, t2_s, t2_r)

    @pl.loop(0, slots)
    def _(s):
        c0 = pl.multiple_of(s * 128, 128)
        wT[:, pl.ds(c0, 128)] = wbf[pl.ds(c0, 128), :].T

    tot_mid()
    total = tot_last()
    inv[...] = scale / total

    def errors(q):
        @pl.loop(0, NZ)
        def _(z):
            lanes = pl.ds(pl.multiple_of(z * zrows, zrows), zrows)
            iota = lax.broadcasted_iota(i32, (128, zrows), 0)
            iz = inv[pl.ds(z, 1), :]
            tz = tgt[z]
            for u in range(quart // 128):
                r0 = pl.multiple_of(q * quart + u * 128, 128)
                hit = iota == (tz - r0)
                e = ez[pl.ds(r0, 128), lanes] * iz - jnp.where(hit, scale, 0.0)
                err[pl.ds(r0, 128), lanes] = e.astype(bf16)

    def center_grad(q):
        r0 = pl.multiple_of(q * quart, 128)
        return nn_dot(err[pl.ds(r0, quart), :], xg[...].reshape(NZ * zrows, width))

    yup, ydn = dev(yy + 1, xx, zz, cc), dev(yy + NY - 1, xx, zz, cc)
    q2, qp, qm = (yy + 2) % NY, (yy + 1) % NY, (yy + NY - 1) % NY

    def to_y(src, dst, k, to):
        send(src, dst, ys_s.at[k], ys_r.at[k], to)

    def keep(q, slot):
        g = center_grad(q)
        for p in range(4):
            pt[slot, p] = g[p * piece:(p + 1) * piece].astype(bf16)
        return g

    errors(q2)
    keep(q2, 0)
    for n in range(2):
        to_y(pt.at[0, n], r2.at[n], n, yup)
        to_y(pt.at[0, 2 + n], r2.at[2 + n], 2 + n, ydn)
    errors(qp)
    pf[0] = center_grad(qp)
    for n in range(2):
        pt[1, 2 + n] = pf[0, pl.ds((2 + n) * piece, piece), :].astype(bf16)
    to_y(pt.at[1, 2], rP.at[2], 4, yup)
    errors(qm)
    pf[1] = center_grad(qm)
    for n in range(2):
        pt[2, n] = pf[1, pl.ds(n * piece, piece), :].astype(bf16)
    to_y(pt.at[2, 0], rM.at[0], 5, ydn)
    errors(yy)

    def merge(n):
        landed(r2.at[n], ys_r.at[n])
        pt[1, n] = (pf[0, pl.ds(n * piece, piece), :] + r2[n].astype(f32)).astype(bf16)
        to_y(pt.at[1, n], rP.at[n], 6 + n, yup)
        landed(r2.at[2 + n], ys_r.at[2 + n])
        pt[2, 2 + n] = (pf[1, pl.ds((2 + n) * piece, piece), :] + r2[2 + n].astype(f32)).astype(bf16)
        to_y(pt.at[2, 2 + n], rM.at[2 + n], 8 + n, ydn)

    def own(n):
        for p in (n, 2 + n):
            landed(rP.at[p], ys_r.at[(6 + n) if p < 2 else (4 if n == 0 else 10)])
            landed(rM.at[p], ys_r.at[(8 + n) if p >= 2 else (5 if n == 0 else 11)])
            s = pf[2, pl.ds(p * piece, piece), :] + rP[p].astype(f32) + rM[p].astype(f32)
            gs[yy, p] = s.astype(bf16)
        for p, q in ((n, 2 + n),):
            send(gs.at[yy, p], gs.at[yy, p], yg_s.at[0, p], yg_r.at[0, p], yup)
            send(gs.at[yy, q], gs.at[yy, q], yg_s.at[1, q], yg_r.at[1, q], ydn)
            send(gs.at[yy, q], gs.at[yy, q], yg_s.at[0, q], yg_r.at[0, q], yup)
            send(gs.at[yy, p], gs.at[yy, p], yg_s.at[1, p], yg_r.at[1, p], ydn)

    def onward(n):
        landed(gs.at[qm, n], yg_r.at[0, n])
        send(gs.at[qm, n], gs.at[qm, n], yg_s.at[2, n], yg_r.at[2, n], yup)
        landed(gs.at[qp, 2 + n], yg_r.at[1, 2 + n])
        send(gs.at[qp, 2 + n], gs.at[qp, 2 + n], yg_s.at[2, 2 + n], yg_r.at[2, 2 + n], ydn)

    group2 = NZ // 2

    def row_grad(lo, hi):
        @pl.loop(lo, hi)
        def _(i):
            z = (zz + NZ // 2 + i) % NZ
            lanes = pl.ds(pl.multiple_of(z * zrows, zrows), zrows)
            gx = nn_dot(wT[...], err[:, lanes]).T
            a, b = gx[: zrows // 2], gx[zrows // 2:]
            gown[i] = jnp.where(cc == 0, a, b)
            goth[i] = jnp.where(cc == 0, b, a).astype(bf16)

    def pair(g):
        part = pl.ds(g * group2, group2)
        send(goth.at[part], pr.at[part], pr_s.at[g], pr_r.at[g], sib)

    def rows_x(g):
        part = pl.ds(g * group2, group2)
        landed(pr.at[part], pr_r.at[g])

        @pl.loop(0, group2)
        def _(n):
            i = g * group2 + n
            h = gown[i] + pr[i].astype(f32)
            gown[i] = h
            for x in range(NX):
                xs[g, x, n] = h[x * rows:(x + 1) * rows].astype(bf16)

        for k in (1, 3, 2):
            send(xs.at[g, (xx + k) % NX], xr.at[g, k - 1], xs_s.at[g, k - 1], xs_r.at[g, k - 1], dev(yy, xx + k, zz, cc))

    def rows_z(g):
        for k in range(1, NX):
            landed(xr.at[g, k - 1], xs_r.at[g, k - 1])
        for n in range(group2):
            i = g * group2 + n
            dz = (NZ // 2 + i) % NZ
            h = gown[i, pl.ds(xrow, rows), :]
            for k in range(1, NX):
                h = h + xr[g, k - 1, n].astype(f32)
            if dz == 0:
                gown[i, pl.ds(xrow, rows), :] = h
            else:
                zs[i] = h.astype(bf16)
                send(zs.at[i], zr.at[dz - 1], zs_s.at[dz - 1], zs_r.at[dz - 1], dev(yy, xx, zz + dz, cc))

    pos_mid, pos_last = reduce_plane(pp, p1, p2, p1_s, p1_r, p2_s, p2_r)
    merge(0)
    row_grad(0, group2)
    pair(0)
    to_y(pt.at[1, 3], rP.at[3], 10, yup)
    to_y(pt.at[2, 1], rM.at[1], 11, ydn)
    merge(1)
    pf[2] = center_grad(yy)
    rows_x(0)
    row_grad(group2, group2 + 2)
    own(0)
    row_grad(group2 + 2, NZ)
    pair(1)
    pos_mid()
    own(1)
    rows_x(1)

    ld_mom.wait()
    tile = 32
    stores = []

    def update(q, p0, np, k):
        base = q * quart + p0 * piece

        @pl.loop(0, np * piece // tile)
        def _(i):
            at = pl.multiple_of(i * tile, tile)
            r0 = pl.multiple_of(base + at, tile)
            r = pl.ds(r0, tile)
            g = gs[q, p0 + at // piece, pl.ds(pl.multiple_of(at % piece, tile), tile), :].astype(f32)
            wf = cen[r, :].astype(f32)
            rn = 1.0 / wn[r, :]
            wu = wf * rn
            gw = (g - wu * jnp.sum(wu * g, axis=1, keepdims=True)) * rn
            live = (r0 // 128) < live_count
            v = mom[r, :]
            nv = jnp.where(live, momentum_rate * v + gw, v)
            nw = jnp.where(live, wf - learn_rate * nv, wf).astype(bf16)
            mom[r, :] = nv
            cen[r, :] = nw

        r = pl.ds(pl.multiple_of(base, tile), np * piece)
        for j, (src, dst) in enumerate(((cen, nw_hbm), (mom, nv_hbm))):
            c = pltpu.make_async_copy(src.at[r, :], dst.at[r, :], stsem.at[k, j])
            c.start()
            stores.append(c)

    update(yy, 0, 4, 0)
    onward(0)
    rows_z(0)
    landed(gs.at[qm, 2], yg_r.at[0, 2])
    landed(gs.at[qp, 0], yg_r.at[1, 0])
    for n, (q, p) in enumerate(((qm, 0), (qm, 2), (qp, 0), (qp, 2))):
        update(q, p, 1, 1 + n)
    onward(1)
    landed(gs.at[qm, 3], yg_r.at[0, 3])
    landed(gs.at[qp, 1], yg_r.at[1, 1])
    for n, (q, p) in enumerate(((qm, 1), (qm, 3), (qp, 1), (qp, 3))):
        update(q, p, 1, 5 + n)
    rows_z(1)
    for n, p in enumerate((0, 2)):
        landed(gs.at[q2, p], yg_r.at[2, p])
        update(q2, p, 1, 9 + n)

    gx = gown[NZ // 2, pl.ds(xrow, rows), :]
    for dz in range(1, NZ):
        landed(zr.at[dz - 1], zs_r.at[dz - 1])
        gx = gx + zr[dz - 1].astype(f32)
    eg_ref[...] = (gx - xu * jnp.sum(xu * gx, axis=1, keepdims=True)) / xn
    pos = pos_last()
    all_loss = jnp.log(scale / inv[...]) - (scale * pos - scale * margin)
    inv[...] = all_loss
    line = inv[pl.ds(zz, 1), :]
    mine = jnp.zeros((1, rows), f32)
    for c in range(NC):
        for x in range(NX):
            at = (c * NX + x) * rows
            here = jnp.logical_and(cc == c, xx == x)
            mine = jnp.where(here, line[:, at:at + rows], mine)
    loss_ref[...] = mine

    for n, p in enumerate((1, 3)):
        landed(gs.at[q2, p], yg_r.at[2, p])
        update(q2, p, 1, 11 + n)

    for c in sends:
        c.wait_send()
    for c in stores:
        c.wait()


def store_kernel(*refs):
    n = len(refs) // 2
    ins, outs, sem = refs[:n], refs[n:2 * n], refs[2 * n]
    copies = [pltpu.make_async_copy(a, b, sem.at[k]) for k, (a, b) in enumerate(zip(ins, outs))]
    for c in copies:
        c.start()
    for c in copies:
        c.wait()


def in_hbm(a):
    return pltpu.with_memory_space_constraint(a, pltpu.HBM)


def on_device(embeddings, labels, centers, momentum, block_list, counts):
    rows, width = embeddings.shape
    slots, blk, _ = centers.shape
    cols = slots * blk
    zrows = NC * NX * rows
    group = NZ * zrows
    quart = cols // NY
    piece = quart // 4
    vm, dma = pltpu.VMEM, pltpu.SemaphoreType.DMA
    npeer = NX * NC - 1
    scratch = [
        vm((rows, width), bf16),
        vm((1, rows), i32),
        pltpu.SMEM((slots,), i32),
        vm((cols, width), bf16),
        vm((cols, width), f32),
        vm((cols, width), bf16),
        vm((width, cols), bf16),
        vm((cols, 1), f32),
        vm((NZ, NC, NX * rows, width), bf16),
        vm((NX * NC, 1, 128), i32),
        vm((NZ, NC, 1, 128), i32),
        vm((NZ, 1, zrows), i32),
        vm((cols, group), f32),
        vm((cols, group), bf16),
        vm((NZ, zrows), f32),
        vm((NZ, zrows), f32),
        vm((npeer, NZ, zrows), f32),
        vm((NZ, NZ, zrows), f32),
        vm((npeer, NZ, zrows), f32),
        vm((NZ, NZ, zrows), f32),
        vm((NZ, zrows), f32),
        vm((3, 4, piece, width), bf16),
        vm((3, quart, width), f32),
        vm((NY, 4, piece, width), bf16),
        vm((4, piece, width), bf16),
        vm((4, piece, width), bf16),
        vm((4, piece, width), bf16),
        vm((NZ, NX * rows, width), f32),
        vm((NZ, NX * rows, width), bf16),
        vm((NZ, NX * rows, width), bf16),
        vm((2, NX, NZ // 2, rows, width), bf16),
        vm((2, NX - 1, NZ // 2, rows, width), bf16),
        vm((NZ, rows, width), bf16),
        vm((NZ - 1, rows, width), bf16),
        dma((5,)), dma((13, 2)),
        dma((NZ, NX - 1)), dma((NZ, NX - 1)), dma((2, NX - 1)), dma((2, NX - 1)), dma((npeer,)), dma((npeer,)), dma((NZ - 1,)), dma((NZ - 1,)),
        dma((NZ - 1,)), dma((NZ - 1,)), dma((NZ,)), dma((NZ,)),
        dma((npeer,)), dma((npeer,)), dma((NZ - 1,)), dma((NZ - 1,)),
        dma((npeer,)), dma((npeer,)), dma((NZ - 1,)), dma((NZ - 1,)),
        dma((12,)), dma((12,)), dma((3, 4)), dma((3, 4)), dma((2,)), dma((2,)),
        dma((2, NX - 1)), dma((2, NX - 1)), dma((NZ - 1,)), dma((NZ - 1,)),
    ]
    vmem = pl.BlockSpec(memory_space=pltpu.VMEM)
    hbm = pl.BlockSpec(memory_space=pltpu.HBM)
    place = pl.BlockSpec(memory_space=pl.ANY)
    results = pl.pallas_call(
        kernel,
        out_shape=(
            jax.ShapeDtypeStruct((1, rows), f32),
            jax.ShapeDtypeStruct((rows, width), f32),
            jax.ShapeDtypeStruct((cols, width), bf16),
            jax.ShapeDtypeStruct((cols, width), f32),
        ),
        in_specs=[hbm, hbm, hbm, pl.BlockSpec(memory_space=pltpu.SMEM), hbm, hbm],
        out_specs=(vmem, vmem, place, place),
        scratch_shapes=scratch,
        compiler_params=pltpu.CompilerParams(
            collective_id=0, has_side_effects=True, vmem_limit_bytes=44 * 1024 * 1024
        ),
        name="margin_step",
    )(
        in_hbm(embeddings),
        in_hbm(labels.reshape(1, rows)),
        in_hbm(block_list),
        counts,
        in_hbm(centers.reshape(cols, width)),
        in_hbm(momentum.reshape(cols, width)),
    )
    loss, eg, nw, nv = pl.pallas_call(
        store_kernel,
        out_shape=tuple(jax.ShapeDtypeStruct(r.shape, r.dtype) for r in results),
        in_specs=[place] * len(results),
        out_specs=(hbm,) * len(results),
        scratch_shapes=[dma((len(results),))],
        compiler_params=pltpu.CompilerParams(vmem_limit_bytes=1024 * 1024),
        name="store_results",
    )(*results)
    return (
        loss.reshape(rows),
        eg,
        nw.reshape(centers.shape),
        nv.reshape(momentum.shape),
    )


def solution(mesh):
    return jax.shard_map(
        on_device,
        mesh=mesh,
        in_specs=(
            P(("dp", "center"), None),
            P(("dp", "center")),
            P("center", None, None),
            P("center", None, None),
            P("center"),
            P("center"),
        ),
        out_specs=(
            P(("dp", "center")),
            P(("dp", "center"), None),
            P("center", None, None),
            P("center", None, None),
        ),
        check_vma=False,
    )
```

```python
import math

import jax
import jax.numpy as jnp
from jax import lax
from jax.experimental import pallas as pl
from jax.experimental.pallas import tpu as pltpu
from jax.sharding import PartitionSpec as P

MESH = pl.DeviceIdType.MESH
NX, NZ, NC, NY = 4, 8, 2, 4
f32, bf16, i32 = jnp.float32, jnp.bfloat16, jnp.int32

scale = 64.0
margin = 0.35
momentum_rate = 0.9
learn_rate = 0.1
tiny_eps = 1e-06
log2e = math.log2(math.e)
dead_bias = -1e30


def nt_dot(a, b):
    return lax.dot_general(a, b, (((1,), (1,)), ((), ())), preferred_element_type=f32)


def nn_dot(a, b):
    return lax.dot_general(a, b, (((1,), (0,)), ((), ())), preferred_element_type=f32)


def kernel(
    emb_hbm, lab_hbm, ids_hbm, cnt_ref, cen_hbm, mom_hbm,
    loss_ref, eg_ref, nw_hbm, nv_hbm,
    emb_ref, lab_ref, ids_ref, cen, mom, wbf, wT, wn, xg, labs, labz, tgt, ez, err, tp, pp, t1, t2, p1, p2, inv,
    pt, pf, gs, r2, rP, rM,
    gown, goth, pr, xs, xr, zs, zr,
    ldsem, stsem,
    xa_s, xa_r, xz_s, xz_r, la_s, la_r, lz_s, lz_r, zg_s, zg_r, sb_s, sb_r,
    t1_s, t1_r, t2_s, t2_r, p1_s, p1_r, p2_s, p2_r,
    ys_s, ys_r, yg_s, yg_r, pr_s, pr_r, xs_s, xs_r, zs_s, zs_r,
):
    rows = emb_ref.shape[0]
    width = emb_ref.shape[1]
    cols = cen.shape[0]
    quart = cols // NY
    piece = quart // 4
    slots = cols // 128
    zrows = NC * NX * rows
    yy = lax.axis_index("dp")
    ce = lax.axis_index("center")
    xx = ce // (NZ * NC)
    zz = (ce // NC) % NZ
    cc = ce % NC

    def dev(y, x, z, c):
        return (y % NY, ((x % NX) * NZ + z % NZ) * NC + c)

    def copy(src, dst, ssem, rsem, to):
        return pltpu.make_async_remote_copy(
            src_ref=src, dst_ref=dst, send_sem=ssem, recv_sem=rsem, device_id=to, device_id_type=MESH
        )

    me = (yy, ce)
    sib = dev(yy, xx, zz, 1 - cc)

    def landed(dst, rsem):
        copy(dst, dst, rsem, rsem, sib).wait_recv()

    xc_peers = [(dx, dc) for dx in range(NX) for dc in range(NC) if (dx, dc) != (0, 0)]
    sends = []

    def send(src, dst, ssem, rsem, to):
        c = copy(src, dst, ssem, rsem, to)
        c.start()
        sends.append(c)

    ld_cen = pltpu.make_async_copy(cen_hbm, cen, ldsem.at[0])
    ld_mom = pltpu.make_async_copy(mom_hbm, mom, ldsem.at[1])
    small = [
        pltpu.make_async_copy(a, b, ldsem.at[2 + k])
        for k, (a, b) in enumerate(
            ((emb_hbm, emb_ref), (lab_hbm, lab_ref), (ids_hbm, ids_ref))
        )
    ]
    for c in small:
        c.start()
    ld_cen.start()
    ld_mom.start()
    barrier = pltpu.get_barrier_semaphore()
    greet = [dev(yy, xx + dx, zz, (cc + dc) % NC) for dx, dc in xc_peers]
    greet += [dev(yy, xx, zz + dz, cc) for dz in range(1, NZ)]
    greet += [dev(yy + 1, xx, zz, cc), dev(yy + NY - 1, xx, zz, cc)]
    for d in greet:
        pl.semaphore_signal(barrier, inc=1, device_id=d, device_id_type=MESH)

    for c in small:
        c.wait()
    xf = emb_ref[...].astype(f32)
    xn = jnp.sqrt(jnp.sum(xf * xf, axis=1, keepdims=True) + tiny_eps)
    xu = xf / xn
    xrow = pl.multiple_of(xx * rows, rows)
    xg[zz, cc, pl.ds(xrow, rows), :] = xu.astype(bf16)
    lab = jnp.concatenate([lab_ref[...]] * NX, axis=1)
    lane = lax.broadcasted_iota(i32, (1, 128), 1)
    labs[0] = jnp.where(lane // rows == xx, lab, 0)
    pl.semaphore_wait(barrier, len(greet))

    def block(dz, dx):
        return xg.at[(zz + NZ - dz) % NZ, cc, pl.ds(pl.multiple_of(((xx + NX - dx) % NX) * rows, rows), rows), :]

    def along_x(dz):
        for k in (1, 3, 2):
            send(block(dz, 0), block(dz, 0), xa_s.at[dz, k - 1], xa_r.at[dz, k - 1], dev(yy, xx + k, zz, cc))

    def along_z(*steps):
        for dz in steps:
            send(block(0, 0), block(0, 0), zg_s.at[dz - 1], zg_r.at[dz - 1], dev(yy, xx, zz + dz, cc))

    along_z(2, 6)
    along_x(0)
    along_z(1, 7)
    for k, (dx, dc) in enumerate(xc_peers):
        send(labs.at[0], labs.at[dx * NC + dc], la_s.at[k], la_r.at[k], dev(yy, xx + dx, zz, (cc + dc) % NC))

    ld_cen.wait()

    @pl.loop(0, slots)
    def _(s):
        r = pl.ds(pl.multiple_of(s * 128, 128), 128)
        wf = cen[r, :].astype(f32)
        n = jnp.sqrt(jnp.sum(wf * wf, axis=1, keepdims=True) + tiny_eps)
        wn[r, :] = n
        wbf[r, :] = (wf * (1.0 / n)).astype(bf16)

    along_z(3, 5, 4)

    def forward(dz):
        landed(block(dz, 0), zg_r.at[dz - 1])
        along_x(dz)

    def neighbours():
        for k in (1, 3, 2):
            landed(block(0, k), xa_r.at[0, k - 1])
            for w, dz in ((0, 1), (1, NZ - 1)):
                send(block(0, k), block(0, k), xz_s.at[w, k - 1], xz_r.at[w, k - 1], dev(yy, xx, zz + dz, cc))

    def share(dz):
        if dz in (1, NZ - 1):
            landed(block(dz, 0), zg_r.at[dz - 1])
        for k in (1, 3, 2):
            if dz in (1, NZ - 1):
                landed(block(dz, k), xz_r.at[int(dz != 1), k - 1])
            elif dz:
                landed(block(dz, k), xa_r.at[dz, k - 1])
        p = xg.at[(zz + NZ - dz) % NZ, cc]
        send(p, p, sb_s.at[dz], sb_r.at[dz], sib)

    neighbours()
    share(0)

    for k, (dx, dc) in enumerate(xc_peers):
        landed(labs.at[dx * NC + dc], la_r.at[k])
    same, other = labs[0], labs[1]
    for dx in range(1, NX):
        same = same + labs[dx * NC]
        other = other + labs[dx * NC + 1]
    labz[zz, 0] = jnp.where(cc == 0, same, other)
    labz[zz, 1] = jnp.where(cc == 0, other, same)
    for dz in (1, 7, 2, 6, 3, 5, 4):
        send(labz.at[zz], labz.at[zz], lz_s.at[dz - 1], lz_r.at[dz - 1], dev(yy, xx, zz + dz, cc))

    def targets(z):
        lb = jnp.concatenate([labz[z, 0], labz[z, 1]], axis=1)
        blk_id = lb // 128
        t = jnp.full(lb.shape, -1, i32)
        for s in range(slots):
            t = jnp.where(blk_id == ids_ref[s], s * 128 + lb % 128, t)
        tgt[z] = t
        return t

    live_count = cnt_ref[0]
    k2 = scale * log2e
    hit_bias = -scale * margin * log2e
    group = 4 if slots % 4 == 0 else 1

    def first_pass(dz):
        z = (zz + NZ - dz) % NZ
        landed(xg.at[z, 1 - cc], sb_r.at[dz])
        if dz:
            landed(labz.at[z], lz_r.at[dz - 1])
        xc = xg[z].reshape(zrows, width)
        tz = targets(z)
        iota = lax.broadcasted_iota(i32, (128, zrows), 0)
        lanes = pl.ds(pl.multiple_of(z * zrows, zrows), zrows)

        def body(g, carry):
            tot, pos = carry
            r0 = pl.multiple_of(g * (group * 128), 128)
            s = nt_dot(wbf[pl.ds(r0, group * 128), :], xc)
            for u in range(group):
                slot = g * group + u
                su = s[u * 128:(u + 1) * 128]
                hit = iota == (tz - slot * 128)
                bias = jnp.where(slot < live_count, 0.0, dead_bias)
                e = jnp.exp2(su * k2 + jnp.where(hit, hit_bias, bias))
                ez[pl.ds(r0 + u * 128, 128), lanes] = e
                tot = tot + jnp.sum(e, axis=0, keepdims=True)
                pos = pos + jnp.sum(jnp.where(hit, su, 0.0), axis=0, keepdims=True)
            return tot, pos

        zero = jnp.zeros((1, zrows), f32)
        tot, pos = lax.fori_loop(0, slots // group, body, (zero, zero))
        tp[pl.ds(z, 1), :] = tot
        pp[pl.ds(z, 1), :] = pos

    forward(2)
    forward(6)
    first_pass(0)
    forward(3)
    forward(5)
    forward(4)
    share(1)
    share(7)
    first_pass(1)
    share(2)
    share(6)
    first_pass(7)
    first_pass(2)
    share(3)
    share(5)
    first_pass(6)
    share(4)
    first_pass(3)
    first_pass(5)
    first_pass(4)

    def reduce_plane(part, near, second, s1, r1, s2, r2):
        for k, (dx, dc) in enumerate(xc_peers):
            send(part, near.at[k], s1.at[k], r1.at[k], dev(yy, xx + dx, zz, (cc + dc) % NC))

        def middle():
            acc = part[...]
            for k in range(len(xc_peers)):
                landed(near.at[k], r1.at[k])
                acc = acc + near[k]
            second[0] = acc
            for dz in range(1, NZ):
                send(second.at[0], second.at[dz], s2.at[dz - 1], r2.at[dz - 1], dev(yy, xx, zz + dz, cc))

        def last():
            acc = second[0]
            for dz in range(1, NZ):
                landed(second.at[dz], r2.at[dz - 1])
                acc = acc + second[dz]
            return acc

        return middle, last

    tot_mid, tot_last = reduce_plane(tp, t1, t2, t1_s, t1_r, t2_s, t2_r)

    @pl.loop(0, slots)
    def _(s):
        c0 = pl.multiple_of(s * 128, 128)
        wT[:, pl.ds(c0, 128)] = wbf[pl.ds(c0, 128), :].T

    tot_mid()
    total = tot_last()
    inv[...] = scale / total

    def errors(q):
        @pl.loop(0, NZ)
        def _(z):
            lanes = pl.ds(pl.multiple_of(z * zrows, zrows), zrows)
            iota = lax.broadcasted_iota(i32, (128, zrows), 0)
            iz = inv[pl.ds(z, 1), :]
            tz = tgt[z]
            for u in range(quart // 128):
                r0 = pl.multiple_of(q * quart + u * 128, 128)
                hit = iota == (tz - r0)
                e = ez[pl.ds(r0, 128), lanes] * iz - jnp.where(hit, scale, 0.0)
                err[pl.ds(r0, 128), lanes] = e.astype(bf16)

    def center_grad(q):
        r0 = pl.multiple_of(q * quart, 128)
        return nn_dot(err[pl.ds(r0, quart), :], xg[...].reshape(NZ * zrows, width))

    yup, ydn = dev(yy + 1, xx, zz, cc), dev(yy + NY - 1, xx, zz, cc)
    q2, qp, qm = (yy + 2) % NY, (yy + 1) % NY, (yy + NY - 1) % NY

    def to_y(src, dst, k, to):
        send(src, dst, ys_s.at[k], ys_r.at[k], to)

    def keep(q, slot):
        g = center_grad(q)
        for p in range(4):
            pt[slot, p] = g[p * piece:(p + 1) * piece].astype(bf16)
        return g

    errors(q2)
    keep(q2, 0)
    for n in range(2):
        to_y(pt.at[0, n], r2.at[n], n, yup)
        to_y(pt.at[0, 2 + n], r2.at[2 + n], 2 + n, ydn)
    errors(qp)
    pf[0] = center_grad(qp)
    for n in range(2):
        pt[1, 2 + n] = pf[0, pl.ds((2 + n) * piece, piece), :].astype(bf16)
    to_y(pt.at[1, 2], rP.at[2], 4, yup)
    errors(qm)
    pf[1] = center_grad(qm)
    for n in range(2):
        pt[2, n] = pf[1, pl.ds(n * piece, piece), :].astype(bf16)
    to_y(pt.at[2, 0], rM.at[0], 5, ydn)
    errors(yy)

    def merge(n):
        landed(r2.at[n], ys_r.at[n])
        pt[1, n] = (pf[0, pl.ds(n * piece, piece), :] + r2[n].astype(f32)).astype(bf16)
        to_y(pt.at[1, n], rP.at[n], 6 + n, yup)
        landed(r2.at[2 + n], ys_r.at[2 + n])
        pt[2, 2 + n] = (pf[1, pl.ds((2 + n) * piece, piece), :] + r2[2 + n].astype(f32)).astype(bf16)
        to_y(pt.at[2, 2 + n], rM.at[2 + n], 8 + n, ydn)

    def own(n):
        for p in (n, 2 + n):
            landed(rP.at[p], ys_r.at[(6 + n) if p < 2 else (4 if n == 0 else 10)])
            landed(rM.at[p], ys_r.at[(8 + n) if p >= 2 else (5 if n == 0 else 11)])
            s = pf[2, pl.ds(p * piece, piece), :] + rP[p].astype(f32) + rM[p].astype(f32)
            gs[yy, p] = s.astype(bf16)
        for p, q in ((n, 2 + n),):
            send(gs.at[yy, p], gs.at[yy, p], yg_s.at[0, p], yg_r.at[0, p], yup)
            send(gs.at[yy, q], gs.at[yy, q], yg_s.at[1, q], yg_r.at[1, q], ydn)
            send(gs.at[yy, q], gs.at[yy, q], yg_s.at[0, q], yg_r.at[0, q], yup)
            send(gs.at[yy, p], gs.at[yy, p], yg_s.at[1, p], yg_r.at[1, p], ydn)

    def onward(n):
        landed(gs.at[qm, n], yg_r.at[0, n])
        send(gs.at[qm, n], gs.at[qm, n], yg_s.at[2, n], yg_r.at[2, n], yup)
        landed(gs.at[qp, 2 + n], yg_r.at[1, 2 + n])
        send(gs.at[qp, 2 + n], gs.at[qp, 2 + n], yg_s.at[2, 2 + n], yg_r.at[2, 2 + n], ydn)

    group2 = 2
    first = 2

    def row_grad(lo, hi):
        @pl.loop(lo, hi)
        def _(i):
            z = (zz + first + i) % NZ
            lanes = pl.ds(pl.multiple_of(z * zrows, zrows), zrows)
            gx = nn_dot(wT[...], err[:, lanes]).T
            a, b = gx[: zrows // 2], gx[zrows // 2:]
            gown[i] = jnp.where(cc == 0, a, b)
            goth[i] = jnp.where(cc == 0, b, a).astype(bf16)

    def pair(g):
        part = pl.ds(g * group2, group2)
        send(goth.at[part], pr.at[part], pr_s.at[g], pr_r.at[g], sib)

    def rows_x(g):
        part = pl.ds(g * group2, group2)
        landed(pr.at[part], pr_r.at[g])

        @pl.loop(0, group2)
        def _(n):
            i = g * group2 + n
            h = gown[i] + pr[i].astype(f32)
            gown[i] = h
            for x in range(NX):
                xs[g, x, n] = h[x * rows:(x + 1) * rows].astype(bf16)

        for k in (1, 3, 2):
            send(xs.at[g, (xx + k) % NX], xr.at[g, k - 1], xs_s.at[g, k - 1], xs_r.at[g, k - 1], dev(yy, xx + k, zz, cc))

    def rows_z(g):
        for k in range(1, NX):
            landed(xr.at[g, k - 1], xs_r.at[g, k - 1])
        for n in range(group2):
            i = g * group2 + n
            dz = (first + i) % NZ
            h = gown[i, pl.ds(xrow, rows), :]
            for k in range(1, NX):
                h = h + xr[g, k - 1, n].astype(f32)
            if dz == 0:
                gown[i, pl.ds(xrow, rows), :] = h
            else:
                zs[i] = h.astype(bf16)
                send(zs.at[i], zr.at[dz - 1], zs_s.at[dz - 1], zs_r.at[dz - 1], dev(yy, xx, zz + dz, cc))

    pos_mid, pos_last = reduce_plane(pp, p1, p2, p1_s, p1_r, p2_s, p2_r)
    row_grad(0, 2)
    pair(0)
    merge(0)
    row_grad(2, 4)
    pair(1)
    rows_x(0)
    to_y(pt.at[1, 3], rP.at[3], 10, yup)
    to_y(pt.at[2, 1], rM.at[1], 11, ydn)
    merge(1)
    row_grad(4, 6)
    pair(2)
    rows_x(1)
    pf[2] = center_grad(yy)
    own(0)
    row_grad(6, 8)
    pair(3)
    rows_x(2)
    pos_mid()
    rows_x(3)
    own(1)
    rows_z(0)

    ld_mom.wait()
    tile = 32
    stores = []

    def update(q, p0, np, k):
        base = q * quart + p0 * piece

        @pl.loop(0, np * piece // tile)
        def _(i):
            at = pl.multiple_of(i * tile, tile)
            r0 = pl.multiple_of(base + at, tile)
            r = pl.ds(r0, tile)
            g = gs[q, p0 + at // piece, pl.ds(pl.multiple_of(at % piece, tile), tile), :].astype(f32)
            wf = cen[r, :].astype(f32)
            rn = 1.0 / wn[r, :]
            wu = wf * rn
            gw = (g - wu * jnp.sum(wu * g, axis=1, keepdims=True)) * rn
            live = (r0 // 128) < live_count
            v = mom[r, :]
            nv = jnp.where(live, momentum_rate * v + gw, v)
            nw = jnp.where(live, wf - learn_rate * nv, wf).astype(bf16)
            mom[r, :] = nv
            cen[r, :] = nw

        r = pl.ds(pl.multiple_of(base, tile), np * piece)
        for j, (src, dst) in enumerate(((cen, nw_hbm), (mom, nv_hbm))):
            c = pltpu.make_async_copy(src.at[r, :], dst.at[r, :], stsem.at[k, j])
            c.start()
            stores.append(c)

    update(yy, 0, 4, 0)
    rows_z(1)
    onward(0)
    landed(gs.at[qm, 2], yg_r.at[0, 2])
    landed(gs.at[qp, 0], yg_r.at[1, 0])
    for n, (q, p) in enumerate(((qm, 0), (qm, 2))):
        update(q, p, 1, 1 + n)
    rows_z(2)
    for n, (q, p) in enumerate(((qp, 0), (qp, 2))):
        update(q, p, 1, 3 + n)
    rows_z(3)
    onward(1)
    landed(gs.at[qm, 3], yg_r.at[0, 3])
    landed(gs.at[qp, 1], yg_r.at[1, 1])
    for n, (q, p) in enumerate(((qm, 1), (qm, 3), (qp, 1), (qp, 3))):
        update(q, p, 1, 5 + n)
    for n, p in enumerate((0, 2)):
        landed(gs.at[q2, p], yg_r.at[2, p])
        update(q2, p, 1, 9 + n)

    gx = gown[NZ - first, pl.ds(xrow, rows), :]
    for dz in range(1, NZ):
        landed(zr.at[dz - 1], zs_r.at[dz - 1])
        gx = gx + zr[dz - 1].astype(f32)
    eg_ref[...] = (gx - xu * jnp.sum(xu * gx, axis=1, keepdims=True)) / xn
    pos = pos_last()
    all_loss = jnp.log(scale / inv[...]) - (scale * pos - scale * margin)
    inv[...] = all_loss
    line = inv[pl.ds(zz, 1), :]
    mine = jnp.zeros((1, rows), f32)
    for c in range(NC):
        for x in range(NX):
            at = (c * NX + x) * rows
            here = jnp.logical_and(cc == c, xx == x)
            mine = jnp.where(here, line[:, at:at + rows], mine)
    loss_ref[...] = mine

    for n, p in enumerate((1, 3)):
        landed(gs.at[q2, p], yg_r.at[2, p])
        update(q2, p, 1, 11 + n)

    for c in sends:
        c.wait_send()
    for c in stores:
        c.wait()


def store_kernel(*refs):
    n = len(refs) // 2
    ins, outs, sem = refs[:n], refs[n:2 * n], refs[2 * n]
    copies = [pltpu.make_async_copy(a, b, sem.at[k]) for k, (a, b) in enumerate(zip(ins, outs))]
    for c in copies:
        c.start()
    for c in copies:
        c.wait()


def in_hbm(a):
    return pltpu.with_memory_space_constraint(a, pltpu.HBM)


def on_device(embeddings, labels, centers, momentum, block_list, counts):
    rows, width = embeddings.shape
    slots, blk, _ = centers.shape
    cols = slots * blk
    zrows = NC * NX * rows
    group = NZ * zrows
    quart = cols // NY
    piece = quart // 4
    vm, dma = pltpu.VMEM, pltpu.SemaphoreType.DMA
    npeer = NX * NC - 1
    scratch = [
        vm((rows, width), bf16),
        vm((1, rows), i32),
        pltpu.SMEM((slots,), i32),
        vm((cols, width), bf16),
        vm((cols, width), f32),
        vm((cols, width), bf16),
        vm((width, cols), bf16),
        vm((cols, 1), f32),
        vm((NZ, NC, NX * rows, width), bf16),
        vm((NX * NC, 1, 128), i32),
        vm((NZ, NC, 1, 128), i32),
        vm((NZ, 1, zrows), i32),
        vm((cols, group), f32),
        vm((cols, group), bf16),
        vm((NZ, zrows), f32),
        vm((NZ, zrows), f32),
        vm((npeer, NZ, zrows), f32),
        vm((NZ, NZ, zrows), f32),
        vm((npeer, NZ, zrows), f32),
        vm((NZ, NZ, zrows), f32),
        vm((NZ, zrows), f32),
        vm((3, 4, piece, width), bf16),
        vm((3, quart, width), f32),
        vm((NY, 4, piece, width), bf16),
        vm((4, piece, width), bf16),
        vm((4, piece, width), bf16),
        vm((4, piece, width), bf16),
        vm((NZ, NX * rows, width), f32),
        vm((NZ, NX * rows, width), bf16),
        vm((NZ, NX * rows, width), bf16),
        vm((4, NX, NZ // 4, rows, width), bf16),
        vm((4, NX - 1, NZ // 4, rows, width), bf16),
        vm((NZ, rows, width), bf16),
        vm((NZ - 1, rows, width), bf16),
        dma((5,)), dma((13, 2)),
        dma((NZ, NX - 1)), dma((NZ, NX - 1)), dma((2, NX - 1)), dma((2, NX - 1)), dma((npeer,)), dma((npeer,)), dma((NZ - 1,)), dma((NZ - 1,)),
        dma((NZ - 1,)), dma((NZ - 1,)), dma((NZ,)), dma((NZ,)),
        dma((npeer,)), dma((npeer,)), dma((NZ - 1,)), dma((NZ - 1,)),
        dma((npeer,)), dma((npeer,)), dma((NZ - 1,)), dma((NZ - 1,)),
        dma((12,)), dma((12,)), dma((3, 4)), dma((3, 4)), dma((4,)), dma((4,)),
        dma((4, NX - 1)), dma((4, NX - 1)), dma((NZ - 1,)), dma((NZ - 1,)),
    ]
    vmem = pl.BlockSpec(memory_space=pltpu.VMEM)
    hbm = pl.BlockSpec(memory_space=pltpu.HBM)
    place = pl.BlockSpec(memory_space=pl.ANY)
    results = pl.pallas_call(
        kernel,
        out_shape=(
            jax.ShapeDtypeStruct((1, rows), f32),
            jax.ShapeDtypeStruct((rows, width), f32),
            jax.ShapeDtypeStruct((cols, width), bf16),
            jax.ShapeDtypeStruct((cols, width), f32),
        ),
        in_specs=[hbm, hbm, hbm, pl.BlockSpec(memory_space=pltpu.SMEM), hbm, hbm],
        out_specs=(vmem, vmem, place, place),
        scratch_shapes=scratch,
        compiler_params=pltpu.CompilerParams(
            collective_id=0, has_side_effects=True, vmem_limit_bytes=44 * 1024 * 1024
        ),
        name="margin_step",
    )(
        in_hbm(embeddings),
        in_hbm(labels.reshape(1, rows)),
        in_hbm(block_list),
        counts,
        in_hbm(centers.reshape(cols, width)),
        in_hbm(momentum.reshape(cols, width)),
    )
    loss, eg, nw, nv = pl.pallas_call(
        store_kernel,
        out_shape=tuple(jax.ShapeDtypeStruct(r.shape, r.dtype) for r in results),
        in_specs=[place] * len(results),
        out_specs=(hbm,) * len(results),
        scratch_shapes=[dma((len(results),))],
        compiler_params=pltpu.CompilerParams(vmem_limit_bytes=1024 * 1024),
        name="store_results",
    )(*results)
    return (
        loss.reshape(rows),
        eg,
        nw.reshape(centers.shape),
        nv.reshape(momentum.shape),
    )


def solution(mesh):
    return jax.shard_map(
        on_device,
        mesh=mesh,
        in_specs=(
            P(("dp", "center"), None),
            P(("dp", "center")),
            P("center", None, None),
            P("center", None, None),
            P("center"),
            P("center"),
        ),
        out_specs=(
            P(("dp", "center")),
            P(("dp", "center"), None),
            P("center", None, None),
            P("center", None, None),
        ),
        check_vma=False,
    )
```

```python
import math

import jax
import jax.numpy as jnp
from jax import lax
from jax.experimental import pallas as pl
from jax.experimental.pallas import tpu as pltpu
from jax.sharding import PartitionSpec as P

MESH = pl.DeviceIdType.MESH
NX, NZ, NC, NY = 4, 8, 2, 4
f32, bf16, i32 = jnp.float32, jnp.bfloat16, jnp.int32

scale = 64.0
margin = 0.35
momentum_rate = 0.9
learn_rate = 0.1
tiny_eps = 1e-06
log2e = math.log2(math.e)
dead_bias = -1e30


def nt_dot(a, b):
    return lax.dot_general(a, b, (((1,), (1,)), ((), ())), preferred_element_type=f32)


def nn_dot(a, b):
    return lax.dot_general(a, b, (((1,), (0,)), ((), ())), preferred_element_type=f32)


def kernel(
    emb_hbm, lab_hbm, ids_hbm, cnt_ref, cen_hbm, mom_hbm,
    loss_ref, eg_ref, nw_hbm, nv_hbm,
    emb_ref, lab_ref, ids_ref, cen, mom, wbf, wT, wn, xg, labs, labz, tgt, ez, err, tp, pp, t1, t2, p1, p2, inv,
    pt, pf, gs, r2, rP, rM,
    gown, goth, pr, xs, xr, zs, zr,
    ldsem, stsem,
    xa_s, xa_r, xz_s, xz_r, la_s, la_r, lz_s, lz_r, zg_s, zg_r, sb_s, sb_r,
    t1_s, t1_r, t2_s, t2_r, p1_s, p1_r, p2_s, p2_r,
    ys_s, ys_r, yg_s, yg_r, pr_s, pr_r, xs_s, xs_r, zs_s, zs_r,
):
    rows = emb_ref.shape[0]
    width = emb_ref.shape[1]
    cols = cen.shape[0]
    quart = cols // NY
    piece = quart // 4
    slots = cols // 128
    zrows = NC * NX * rows
    yy = lax.axis_index("dp")
    ce = lax.axis_index("center")
    xx = ce // (NZ * NC)
    zz = (ce // NC) % NZ
    cc = ce % NC

    def dev(y, x, z, c):
        return (y % NY, ((x % NX) * NZ + z % NZ) * NC + c)

    def copy(src, dst, ssem, rsem, to):
        return pltpu.make_async_remote_copy(
            src_ref=src, dst_ref=dst, send_sem=ssem, recv_sem=rsem, device_id=to, device_id_type=MESH
        )

    me = (yy, ce)
    sib = dev(yy, xx, zz, 1 - cc)

    def landed(dst, rsem):
        copy(dst, dst, rsem, rsem, sib).wait_recv()

    xc_peers = [(dx, dc) for dx in range(NX) for dc in range(NC) if (dx, dc) != (0, 0)]
    sends = []

    def send(src, dst, ssem, rsem, to):
        c = copy(src, dst, ssem, rsem, to)
        c.start()
        sends.append(c)

    ld_cen = pltpu.make_async_copy(cen_hbm, cen, ldsem.at[0])
    ld_mom = pltpu.make_async_copy(mom_hbm, mom, ldsem.at[1])
    small = [
        pltpu.make_async_copy(a, b, ldsem.at[2 + k])
        for k, (a, b) in enumerate(
            ((emb_hbm, emb_ref), (lab_hbm, lab_ref), (ids_hbm, ids_ref))
        )
    ]
    for c in small:
        c.start()
    ld_cen.start()
    ld_mom.start()
    barrier = pltpu.get_barrier_semaphore()
    greet = [dev(yy, xx + dx, zz, (cc + dc) % NC) for dx, dc in xc_peers]
    greet += [dev(yy, xx, zz + dz, cc) for dz in range(1, NZ)]
    greet += [dev(yy + 1, xx, zz, cc), dev(yy + NY - 1, xx, zz, cc)]
    for d in greet:
        pl.semaphore_signal(barrier, inc=1, device_id=d, device_id_type=MESH)

    for c in small:
        c.wait()
    xf = emb_ref[...].astype(f32)
    xn = jnp.sqrt(jnp.sum(xf * xf, axis=1, keepdims=True) + tiny_eps)
    xu = xf / xn
    xrow = pl.multiple_of(xx * rows, rows)
    xg[zz, cc, pl.ds(xrow, rows), :] = xu.astype(bf16)
    lab = jnp.concatenate([lab_ref[...]] * NX, axis=1)
    lane = lax.broadcasted_iota(i32, (1, 128), 1)
    labs[0] = jnp.where(lane // rows == xx, lab, 0)
    pl.semaphore_wait(barrier, len(greet))

    def block(dz, dx):
        return xg.at[(zz + NZ - dz) % NZ, cc, pl.ds(pl.multiple_of(((xx + NX - dx) % NX) * rows, rows), rows), :]

    def along_x(dz):
        for k in (1, 3, 2):
            send(block(dz, 0), block(dz, 0), xa_s.at[dz, k - 1], xa_r.at[dz, k - 1], dev(yy, xx + k, zz, cc))

    def along_z(*steps):
        for dz in steps:
            send(block(0, 0), block(0, 0), zg_s.at[dz - 1], zg_r.at[dz - 1], dev(yy, xx, zz + dz, cc))

    along_z(2, 6)
    along_x(0)
    along_z(1, 7)
    for k, (dx, dc) in enumerate(xc_peers):
        send(labs.at[0], labs.at[dx * NC + dc], la_s.at[k], la_r.at[k], dev(yy, xx + dx, zz, (cc + dc) % NC))

    ld_cen.wait()

    @pl.loop(0, slots)
    def _(s):
        r = pl.ds(pl.multiple_of(s * 128, 128), 128)
        wf = cen[r, :].astype(f32)
        n = jnp.sqrt(jnp.sum(wf * wf, axis=1, keepdims=True) + tiny_eps)
        wn[r, :] = n
        wbf[r, :] = (wf * (1.0 / n)).astype(bf16)

    along_z(3, 5, 4)

    def forward(dz):
        landed(block(dz, 0), zg_r.at[dz - 1])
        along_x(dz)

    def neighbours():
        for k in (1, 3, 2):
            landed(block(0, k), xa_r.at[0, k - 1])
            for w, dz in ((0, 1), (1, NZ - 1)):
                send(block(0, k), block(0, k), xz_s.at[w, k - 1], xz_r.at[w, k - 1], dev(yy, xx, zz + dz, cc))

    def share(dz):
        if dz in (1, NZ - 1):
            landed(block(dz, 0), zg_r.at[dz - 1])
        for k in (1, 3, 2):
            if dz in (1, NZ - 1):
                landed(block(dz, k), xz_r.at[int(dz != 1), k - 1])
            elif dz:
                landed(block(dz, k), xa_r.at[dz, k - 1])
        p = xg.at[(zz + NZ - dz) % NZ, cc]
        send(p, p, sb_s.at[dz], sb_r.at[dz], sib)

    neighbours()
    share(0)

    for k, (dx, dc) in enumerate(xc_peers):
        landed(labs.at[dx * NC + dc], la_r.at[k])
    same, other = labs[0], labs[1]
    for dx in range(1, NX):
        same = same + labs[dx * NC]
        other = other + labs[dx * NC + 1]
    labz[zz, 0] = jnp.where(cc == 0, same, other)
    labz[zz, 1] = jnp.where(cc == 0, other, same)
    for dz in (1, 7, 2, 6, 3, 5, 4):
        send(labz.at[zz], labz.at[zz], lz_s.at[dz - 1], lz_r.at[dz - 1], dev(yy, xx, zz + dz, cc))

    def targets(z):
        lb = jnp.concatenate([labz[z, 0], labz[z, 1]], axis=1)
        blk_id = lb // 128
        t = jnp.full(lb.shape, -1, i32)
        for s in range(slots):
            t = jnp.where(blk_id == ids_ref[s], s * 128 + lb % 128, t)
        tgt[z] = t
        return t

    live_count = cnt_ref[0]
    k2 = scale * log2e
    hit_bias = -scale * margin * log2e
    group = 4 if slots % 4 == 0 else 1

    def first_pass(dz):
        z = (zz + NZ - dz) % NZ
        landed(xg.at[z, 1 - cc], sb_r.at[dz])
        if dz:
            landed(labz.at[z], lz_r.at[dz - 1])
        xc = xg[z].reshape(zrows, width)
        tz = targets(z)
        iota = lax.broadcasted_iota(i32, (128, zrows), 0)
        lanes = pl.ds(pl.multiple_of(z * zrows, zrows), zrows)

        def body(g, carry):
            tot, pos = carry
            r0 = pl.multiple_of(g * (group * 128), 128)
            s = nt_dot(wbf[pl.ds(r0, group * 128), :], xc)
            for u in range(group):
                slot = g * group + u
                su = s[u * 128:(u + 1) * 128]
                hit = iota == (tz - slot * 128)
                bias = jnp.where(slot < live_count, 0.0, dead_bias)
                e = jnp.exp2(su * k2 + jnp.where(hit, hit_bias, bias))
                ez[pl.ds(r0 + u * 128, 128), lanes] = e
                tot = tot + jnp.sum(e, axis=0, keepdims=True)
                pos = pos + jnp.sum(jnp.where(hit, su, 0.0), axis=0, keepdims=True)
            return tot, pos

        zero = jnp.zeros((1, zrows), f32)
        tot, pos = lax.fori_loop(0, slots // group, body, (zero, zero))
        tp[pl.ds(z, 1), :] = tot
        pp[pl.ds(z, 1), :] = pos

    forward(2)
    forward(6)
    first_pass(0)
    forward(3)
    forward(5)
    forward(4)
    share(1)
    share(7)
    first_pass(1)
    share(2)
    share(6)
    first_pass(7)
    first_pass(2)
    share(3)
    share(5)
    first_pass(6)
    share(4)
    first_pass(3)
    first_pass(5)
    first_pass(4)

    def reduce_plane(part, near, second, s1, r1, s2, r2):
        for k, (dx, dc) in enumerate(xc_peers):
            send(part, near.at[k], s1.at[k], r1.at[k], dev(yy, xx + dx, zz, (cc + dc) % NC))

        def middle():
            acc = part[...]
            for k in range(len(xc_peers)):
                landed(near.at[k], r1.at[k])
                acc = acc + near[k]
            second[0] = acc
            for dz in range(1, NZ):
                send(second.at[0], second.at[dz], s2.at[dz - 1], r2.at[dz - 1], dev(yy, xx, zz + dz, cc))

        def last():
            acc = second[0]
            for dz in range(1, NZ):
                landed(second.at[dz], r2.at[dz - 1])
                acc = acc + second[dz]
            return acc

        return middle, last

    tot_mid, tot_last = reduce_plane(tp, t1, t2, t1_s, t1_r, t2_s, t2_r)

    @pl.loop(0, slots)
    def _(s):
        c0 = pl.multiple_of(s * 128, 128)
        wT[:, pl.ds(c0, 128)] = wbf[pl.ds(c0, 128), :].T

    tot_mid()
    total = tot_last()
    inv[...] = scale / total

    def errors(q):
        @pl.loop(0, NZ)
        def _(z):
            lanes = pl.ds(pl.multiple_of(z * zrows, zrows), zrows)
            iota = lax.broadcasted_iota(i32, (128, zrows), 0)
            iz = inv[pl.ds(z, 1), :]
            tz = tgt[z]
            for u in range(quart // 128):
                r0 = pl.multiple_of(q * quart + u * 128, 128)
                hit = iota == (tz - r0)
                e = ez[pl.ds(r0, 128), lanes] * iz - jnp.where(hit, scale, 0.0)
                err[pl.ds(r0, 128), lanes] = e.astype(bf16)

    def center_grad(q):
        r0 = pl.multiple_of(q * quart, 128)
        return nn_dot(err[pl.ds(r0, quart), :], xg[...].reshape(NZ * zrows, width))

    yup, ydn = dev(yy + 1, xx, zz, cc), dev(yy + NY - 1, xx, zz, cc)
    q2, qp, qm = (yy + 2) % NY, (yy + 1) % NY, (yy + NY - 1) % NY

    def to_y(src, dst, k, to):
        send(src, dst, ys_s.at[k], ys_r.at[k], to)

    def keep(q, slot):
        g = center_grad(q)
        for p in range(4):
            pt[slot, p] = g[p * piece:(p + 1) * piece].astype(bf16)
        return g

    errors(q2)
    keep(q2, 0)
    for n in range(2):
        to_y(pt.at[0, n], r2.at[n], n, yup)
        to_y(pt.at[0, 2 + n], r2.at[2 + n], 2 + n, ydn)
    errors(qp)
    pf[0] = center_grad(qp)
    for n in range(2):
        pt[1, 2 + n] = pf[0, pl.ds((2 + n) * piece, piece), :].astype(bf16)
    to_y(pt.at[1, 2], rP.at[2], 4, yup)
    errors(qm)
    pf[1] = center_grad(qm)
    for n in range(2):
        pt[2, n] = pf[1, pl.ds(n * piece, piece), :].astype(bf16)
    to_y(pt.at[2, 0], rM.at[0], 5, ydn)
    errors(yy)

    def merge(n):
        landed(r2.at[n], ys_r.at[n])
        pt[1, n] = (pf[0, pl.ds(n * piece, piece), :] + r2[n].astype(f32)).astype(bf16)
        to_y(pt.at[1, n], rP.at[n], 6 + n, yup)
        landed(r2.at[2 + n], ys_r.at[2 + n])
        pt[2, 2 + n] = (pf[1, pl.ds((2 + n) * piece, piece), :] + r2[2 + n].astype(f32)).astype(bf16)
        to_y(pt.at[2, 2 + n], rM.at[2 + n], 8 + n, ydn)

    def own(n):
        for p in (n, 2 + n):
            landed(rP.at[p], ys_r.at[(6 + n) if p < 2 else (4 if n == 0 else 10)])
            landed(rM.at[p], ys_r.at[(8 + n) if p >= 2 else (5 if n == 0 else 11)])
            s = pf[2, pl.ds(p * piece, piece), :] + rP[p].astype(f32) + rM[p].astype(f32)
            gs[yy, p] = s.astype(bf16)
        spread(0, n, yup)
        spread(1, 2 + n, ydn)

    def spread(way, p, to):
        send(gs.at[yy, p], gs.at[yy, p], yg_s.at[way, p], yg_r.at[way, p], to)

    def rest(n):
        spread(0, 2 + n, yup)
        spread(1, n, ydn)

    def onward(n):
        landed(gs.at[qm, n], yg_r.at[0, n])
        send(gs.at[qm, n], gs.at[qm, n], yg_s.at[2, n], yg_r.at[2, n], yup)
        landed(gs.at[qp, 2 + n], yg_r.at[1, 2 + n])
        send(gs.at[qp, 2 + n], gs.at[qp, 2 + n], yg_s.at[2, 2 + n], yg_r.at[2, 2 + n], ydn)

    group2 = 2
    first = 2

    def row_grad(lo, hi):
        @pl.loop(lo, hi)
        def _(i):
            z = (zz + first + i) % NZ
            lanes = pl.ds(pl.multiple_of(z * zrows, zrows), zrows)
            gx = nn_dot(wT[...], err[:, lanes]).T
            a, b = gx[: zrows // 2], gx[zrows // 2:]
            gown[i] = jnp.where(cc == 0, a, b)
            goth[i] = jnp.where(cc == 0, b, a).astype(bf16)

    def pair(g):
        part = pl.ds(g * group2, group2)
        send(goth.at[part], pr.at[part], pr_s.at[g], pr_r.at[g], sib)

    def rows_x(g):
        part = pl.ds(g * group2, group2)
        landed(pr.at[part], pr_r.at[g])

        @pl.loop(0, group2)
        def _(n):
            i = g * group2 + n
            h = gown[i] + pr[i].astype(f32)
            gown[i] = h
            for x in range(NX):
                xs[g, x, n] = h[x * rows:(x + 1) * rows].astype(bf16)

        for k in (1, 3, 2):
            send(xs.at[g, (xx + k) % NX], xr.at[g, k - 1], xs_s.at[g, k - 1], xs_r.at[g, k - 1], dev(yy, xx + k, zz, cc))

    def rows_z(g):
        for k in range(1, NX):
            landed(xr.at[g, k - 1], xs_r.at[g, k - 1])
        for n in range(group2):
            i = g * group2 + n
            dz = (first + i) % NZ
            h = gown[i, pl.ds(xrow, rows), :]
            for k in range(1, NX):
                h = h + xr[g, k - 1, n].astype(f32)
            if dz == 0:
                gown[i, pl.ds(xrow, rows), :] = h
            else:
                zs[i] = h.astype(bf16)
                send(zs.at[i], zr.at[dz - 1], zs_s.at[dz - 1], zs_r.at[dz - 1], dev(yy, xx, zz + dz, cc))

    pos_mid, pos_last = reduce_plane(pp, p1, p2, p1_s, p1_r, p2_s, p2_r)
    row_grad(0, 2)
    pair(0)
    merge(0)
    row_grad(2, 4)
    pair(1)
    rows_x(0)
    to_y(pt.at[1, 3], rP.at[3], 10, yup)
    to_y(pt.at[2, 1], rM.at[1], 11, ydn)
    merge(1)
    row_grad(4, 6)
    pair(2)
    rows_x(1)
    pf[2] = center_grad(yy)
    own(0)
    row_grad(6, 8)
    pair(3)
    rows_x(2)
    pos_mid()
    rows_x(3)
    own(1)
    rest(0)
    rows_z(0)

    ld_mom.wait()
    tile = 32
    stores = []

    def update(q, p0, np, k):
        base = q * quart + p0 * piece

        @pl.loop(0, np * piece // tile)
        def _(i):
            at = pl.multiple_of(i * tile, tile)
            r0 = pl.multiple_of(base + at, tile)
            r = pl.ds(r0, tile)
            g = gs[q, p0 + at // piece, pl.ds(pl.multiple_of(at % piece, tile), tile), :].astype(f32)
            wf = cen[r, :].astype(f32)
            rn = 1.0 / wn[r, :]
            wu = wf * rn
            gw = (g - wu * jnp.sum(wu * g, axis=1, keepdims=True)) * rn
            live = (r0 // 128) < live_count
            v = mom[r, :]
            nv = jnp.where(live, momentum_rate * v + gw, v)
            nw = jnp.where(live, wf - learn_rate * nv, wf).astype(bf16)
            mom[r, :] = nv
            cen[r, :] = nw

        r = pl.ds(pl.multiple_of(base, tile), np * piece)
        for j, (src, dst) in enumerate(((cen, nw_hbm), (mom, nv_hbm))):
            c = pltpu.make_async_copy(src.at[r, :], dst.at[r, :], stsem.at[k, j])
            c.start()
            stores.append(c)

    update(yy, 0, 4, 0)
    onward(0)
    rest(1)
    rows_z(1)
    for n, (q, p) in enumerate(((qm, 0), (qp, 2))):
        update(q, p, 1, 1 + n)
    rows_z(2)
    onward(1)
    rows_z(3)
    for n, (q, p) in enumerate(((qm, 1), (qp, 3))):
        update(q, p, 1, 3 + n)
    landed(gs.at[qm, 2], yg_r.at[0, 2])
    update(qm, 2, 1, 5)
    landed(gs.at[qp, 0], yg_r.at[1, 0])
    update(qp, 0, 1, 6)
    for n, p in enumerate((0, 2)):
        landed(gs.at[q2, p], yg_r.at[2, p])
        update(q2, p, 1, 7 + n)

    gx = gown[NZ - first, pl.ds(xrow, rows), :]
    for dz in range(1, NZ):
        landed(zr.at[dz - 1], zs_r.at[dz - 1])
        gx = gx + zr[dz - 1].astype(f32)
    eg_ref[...] = (gx - xu * jnp.sum(xu * gx, axis=1, keepdims=True)) / xn
    pos = pos_last()
    all_loss = jnp.log(scale / inv[...]) - (scale * pos - scale * margin)
    inv[...] = all_loss
    line = inv[pl.ds(zz, 1), :]
    mine = jnp.zeros((1, rows), f32)
    for c in range(NC):
        for x in range(NX):
            at = (c * NX + x) * rows
            here = jnp.logical_and(cc == c, xx == x)
            mine = jnp.where(here, line[:, at:at + rows], mine)
    loss_ref[...] = mine

    landed(gs.at[qm, 3], yg_r.at[0, 3])
    update(qm, 3, 1, 9)
    landed(gs.at[qp, 1], yg_r.at[1, 1])
    update(qp, 1, 1, 10)
    for n, p in enumerate((1, 3)):
        landed(gs.at[q2, p], yg_r.at[2, p])
        update(q2, p, 1, 11 + n)

    for c in sends:
        c.wait_send()
    for c in stores:
        c.wait()


def store_kernel(*refs):
    n = len(refs) // 2
    ins, outs, sem = refs[:n], refs[n:2 * n], refs[2 * n]
    copies = [pltpu.make_async_copy(a, b, sem.at[k]) for k, (a, b) in enumerate(zip(ins, outs))]
    for c in copies:
        c.start()
    for c in copies:
        c.wait()


def in_hbm(a):
    return pltpu.with_memory_space_constraint(a, pltpu.HBM)


def on_device(embeddings, labels, centers, momentum, block_list, counts):
    rows, width = embeddings.shape
    slots, blk, _ = centers.shape
    cols = slots * blk
    zrows = NC * NX * rows
    group = NZ * zrows
    quart = cols // NY
    piece = quart // 4
    vm, dma = pltpu.VMEM, pltpu.SemaphoreType.DMA
    npeer = NX * NC - 1
    scratch = [
        vm((rows, width), bf16),
        vm((1, rows), i32),
        pltpu.SMEM((slots,), i32),
        vm((cols, width), bf16),
        vm((cols, width), f32),
        vm((cols, width), bf16),
        vm((width, cols), bf16),
        vm((cols, 1), f32),
        vm((NZ, NC, NX * rows, width), bf16),
        vm((NX * NC, 1, 128), i32),
        vm((NZ, NC, 1, 128), i32),
        vm((NZ, 1, zrows), i32),
        vm((cols, group), f32),
        vm((cols, group), bf16),
        vm((NZ, zrows), f32),
        vm((NZ, zrows), f32),
        vm((npeer, NZ, zrows), f32),
        vm((NZ, NZ, zrows), f32),
        vm((npeer, NZ, zrows), f32),
        vm((NZ, NZ, zrows), f32),
        vm((NZ, zrows), f32),
        vm((3, 4, piece, width), bf16),
        vm((3, quart, width), f32),
        vm((NY, 4, piece, width), bf16),
        vm((4, piece, width), bf16),
        vm((4, piece, width), bf16),
        vm((4, piece, width), bf16),
        vm((NZ, NX * rows, width), f32),
        vm((NZ, NX * rows, width), bf16),
        vm((NZ, NX * rows, width), bf16),
        vm((4, NX, NZ // 4, rows, width), bf16),
        vm((4, NX - 1, NZ // 4, rows, width), bf16),
        vm((NZ, rows, width), bf16),
        vm((NZ - 1, rows, width), bf16),
        dma((5,)), dma((13, 2)),
        dma((NZ, NX - 1)), dma((NZ, NX - 1)), dma((2, NX - 1)), dma((2, NX - 1)), dma((npeer,)), dma((npeer,)), dma((NZ - 1,)), dma((NZ - 1,)),
        dma((NZ - 1,)), dma((NZ - 1,)), dma((NZ,)), dma((NZ,)),
        dma((npeer,)), dma((npeer,)), dma((NZ - 1,)), dma((NZ - 1,)),
        dma((npeer,)), dma((npeer,)), dma((NZ - 1,)), dma((NZ - 1,)),
        dma((12,)), dma((12,)), dma((3, 4)), dma((3, 4)), dma((4,)), dma((4,)),
        dma((4, NX - 1)), dma((4, NX - 1)), dma((NZ - 1,)), dma((NZ - 1,)),
    ]
    vmem = pl.BlockSpec(memory_space=pltpu.VMEM)
    hbm = pl.BlockSpec(memory_space=pltpu.HBM)
    place = pl.BlockSpec(memory_space=pl.ANY)
    results = pl.pallas_call(
        kernel,
        out_shape=(
            jax.ShapeDtypeStruct((1, rows), f32),
            jax.ShapeDtypeStruct((rows, width), f32),
            jax.ShapeDtypeStruct((cols, width), bf16),
            jax.ShapeDtypeStruct((cols, width), f32),
        ),
        in_specs=[hbm, hbm, hbm, pl.BlockSpec(memory_space=pltpu.SMEM), hbm, hbm],
        out_specs=(vmem, vmem, place, place),
        scratch_shapes=scratch,
        compiler_params=pltpu.CompilerParams(
            collective_id=0, has_side_effects=True, vmem_limit_bytes=44 * 1024 * 1024
        ),
        name="margin_step",
    )(
        in_hbm(embeddings),
        in_hbm(labels.reshape(1, rows)),
        in_hbm(block_list),
        counts,
        in_hbm(centers.reshape(cols, width)),
        in_hbm(momentum.reshape(cols, width)),
    )
    loss, eg, nw, nv = pl.pallas_call(
        store_kernel,
        out_shape=tuple(jax.ShapeDtypeStruct(r.shape, r.dtype) for r in results),
        in_specs=[place] * len(results),
        out_specs=(hbm,) * len(results),
        scratch_shapes=[dma((len(results),))],
        compiler_params=pltpu.CompilerParams(vmem_limit_bytes=1024 * 1024),
        name="store_results",
    )(*results)
    return (
        loss.reshape(rows),
        eg,
        nw.reshape(centers.shape),
        nv.reshape(momentum.shape),
    )


def solution(mesh):
    return jax.shard_map(
        on_device,
        mesh=mesh,
        in_specs=(
            P(("dp", "center"), None),
            P(("dp", "center")),
            P("center", None, None),
            P("center", None, None),
            P("center"),
            P("center"),
        ),
        out_specs=(
            P(("dp", "center")),
            P(("dp", "center"), None),
            P("center", None, None),
            P("center", None, None),
        ),
        check_vma=False,
    )
```
